512 devices in a mesh: space: 64 (over z, y), members: 8 (over x, core).
Axes of the slice: x: 4, y: 4, z: 16, core: 2. Of those that a mesh axis runs over, the one named last changes fastest.
Arguments:
- log_field: float32 [512, 8192], P('members', 'space'), may hold values from -6 to 6
- obs_heads: float32 [2048], P('space'), may hold values from -6 to 6
- obs_var: float32 [2048], P('space'), may hold values from 0.05 to 0.5
- obs_noise: float32 [512, 2048], P('members', 'space'), may hold values from -6 to 6
- obs_index: int32 [64, 32], P('space'), may hold values from 0 to 127
- obs_count: int32 [64], P('space'), may hold values from 1 to 32, 1024 in all
- neighbours: int32 [512, 64], P('members'), may hold values from 0 to 511, all different within a row
- lift_gain: float32 [48], replicated, may hold values from -4 to 4
- lift_bias: float32 [48], replicated, may hold values from -3 to 3
- conv_first: bfloat16 [3, 48, 48], replicated, may hold values from -0.5 to 0.5
- bias_first: float32 [48], replicated, may hold values from -2 to 2
- conv_second: bfloat16 [3, 48, 96], replicated, may hold values from -0.375 to 0.375
- bias_second: float32 [48], replicated, may hold values from -2 to 2
- readout: bfloat16 [144], replicated, may hold values from -0.5 to 0.5
Outputs:
- updated_field: float32 [512, 8192], P('members', 'space')
- new_heads: float32 [512, 8192], P('members', 'space')
The draws below stay inside these ranges and needn't reach their ends.
Inputs may be any that keep to these rules, and one draw needn't show every extreme that they name: `obs_index`: cells are counted within the tile that holds the slot. `obs_count`: the counts sum to 1024 and the largest is exactly 32. `neighbours`: each row names 64 different members; every member is named by some row.
All inputs are finite; a program needn't handle non-finite values. No bound on the sum of `obs_count` on one device may be relied on, other than what follows from the above.
Results may differ from the reference program's by a relative error of at most 0.0051.
Values may be sent and summed in bfloat16 or wider, within the bound.
A program may use at most 64 MiB of HBM per device.

```python
import math
import jax
import jax.numpy as jnp
import numpy as np
from jax import lax

CHANNELS = 48
NEIGHBOURS = 64
CELLS_DEV = 128
OBS_CAP = 32
MEMBERS = 512
CELLS = 8192
OBS_TOTAL = 2048
N_SPACE = 64


def with_ends(values, rng, low, top_value):
    longest = values.shape.index(max(values.shape))
    spots = []
    for shift in (0, 1):
        where = [jax.random.randint(jax.random.fold_in(rng, axis), (), 0, length) for axis, length in enumerate(values.shape)]
        where[longest] = (where[longest] + shift) % values.shape[longest]
        spots.append(tuple(where))
    return values.at[spots[0]].set(low).at[spots[1]].set(top_value)


def block_scale(key, extent, cuts, smallest, largest):
    factor_of = 1.0
    for position, parts in cuts:
        draws = jax.random.uniform(jax.random.fold_in(jax.random.fold_in(key, 6), position), (parts,), jnp.float32, smallest / len(cuts), largest / len(cuts))
        factor_of = factor_of * jnp.repeat(jnp.exp(draws), extent[position] // parts).reshape((-1,) + (1,) * (len(extent) - 1 - position))
    return factor_of


def different_ones(own_key, rows, number_of, top, lift):
    order = jax.random.permutation(jax.random.fold_in(own_key, 1), number_of)
    favour = order
    for power in range(3):
        favour = favour * favour // number_of
    favour = favour * lift // number_of
    tickets = jax.random.randint(jax.random.fold_in(own_key, 2), (rows, number_of), 0, 4096) + favour
    sure = jax.random.permutation(jax.random.fold_in(own_key, 3), rows)[jnp.arange(number_of) % rows]
    tickets = jnp.where(jnp.arange(rows)[:, None] == sure[None, :], 1 << 14, tickets)
    score = tickets * number_of + jnp.arange(number_of)
    return lax.top_k(score.astype(jnp.int32), top)[1].astype(jnp.int32)


def split_up(amount, total, bound, skew):
    loads = [(1 << 20) // math.isqrt(rank ** skew) + 1 for rank in range(2, amount + 1)]
    spare, counts = total - bound - (amount - 1), [1] * (amount - 1)
    while spare > 0:
        free = [i for i in range(amount - 1) if counts[i] < bound]
        pool, left = sum([loads[i] for i in free]), spare
        for i in free:
            addition = min(bound - counts[i], max(1, left * loads[i] // pool), spare)
            counts[i] = counts[i] + addition
            spare = spare - addition
    return np.array([bound] + counts)


def uneven(own_key, count, total, reach, slope):
    if count == 2:
        one = jax.random.randint(own_key, (), max(1, total - reach), min(reach, total - 1) + 1)
        return jnp.stack([one, total - one])
    sizes = jnp.asarray(split_up(count, total, reach, slope), jnp.int32)
    couples = (count - 1) // 2
    donor, taker = sizes[1:1 + 2 * couples:2], sizes[2:2 + 2 * couples:2]
    slack = jnp.minimum(donor - 1, reach - taker)
    shifted = jax.random.randint(jax.random.fold_in(own_key, 1), (couples,), 0, 1 << 20) % (slack + 1)
    sizes = sizes.at[1:1 + 2 * couples:2].set(donor - shifted).at[2:2 + 2 * couples:2].set(taker + shifted)
    return sizes[jax.random.permutation(jax.random.fold_in(own_key, 2), count)]


def scatter_about(key, shape, width, bound, pieces=(), held_as=jnp.bfloat16):
    drawn = width * jax.random.normal(key, shape, jnp.float32)
    if pieces:
        drawn = drawn * block_scale(key, shape, pieces, -0.22, 0.18)
    return jnp.clip(drawn, -bound, bound).astype(held_as)


def setup_inputs(seed: int = 0) -> dict:
    splits = jax.random.split(jax.random.key(seed), 15)
    return {
        "log_field": scatter_about(splits[0], (MEMBERS, CELLS), 1.0, 6.0, ((0, 8), (1, 64)), jnp.float32),
        "obs_heads": scatter_about(splits[1], (OBS_TOTAL,), 1.0, 6.0, ((0, 64),), jnp.float32),
        "obs_var": jnp.clip(jnp.exp(math.log(0.5) - 2.3025851 * jax.random.uniform(splits[2], (OBS_TOTAL,), jnp.float32) ** block_scale(splits[2], (OBS_TOTAL,), ((0, 64),), -0.2, 0.2)), 0.05, 0.5),
        "obs_noise": scatter_about(splits[3], (MEMBERS, OBS_TOTAL), 1.0, 6.0, ((0, 8), (1, 64)), jnp.float32),
        "obs_index": with_ends(jax.random.randint(splits[4], (N_SPACE, OBS_CAP), 0, CELLS_DEV), jax.random.fold_in(splits[4], 1), 0, CELLS_DEV - 1).astype(jnp.int32),
        "obs_count": uneven(splits[5], N_SPACE, OBS_TOTAL // 2, OBS_CAP, 2).astype(jnp.int32),
        "neighbours": different_ones(splits[6], MEMBERS, MEMBERS, NEIGHBOURS, 2048),
        "lift_gain": scatter_about(splits[7], (CHANNELS,), 1.0, 4.0, (), jnp.float32),
        "lift_bias": scatter_about(splits[8], (CHANNELS,), 0.5, 3.0, (), jnp.float32),
        "conv_first": scatter_about(splits[9], (3, CHANNELS, CHANNELS), (3 * CHANNELS) ** -0.5, 0.5),
        "bias_first": scatter_about(splits[10], (CHANNELS,), 0.3, 2.0, (), jnp.float32),
        "conv_second": scatter_about(splits[11], (3, CHANNELS, 2 * CHANNELS), (6 * CHANNELS) ** -0.5, 0.375),
        "bias_second": scatter_about(splits[12], (CHANNELS,), 0.3, 2.0, (), jnp.float32),
        "readout": scatter_about(splits[13], (3 * CHANNELS,), (3 * CHANNELS) ** -0.5, 0.5),
    }


def dilated_conv(padded_input, kernel_taps, kernel_bias, dilation, width_cells):
    total_sum = jnp.zeros((kernel_taps.shape[1], padded_input.shape[1], width_cells), jnp.float32)
    for kernel_tap in range(3):
        window_cells = lax.slice_in_dim(padded_input, kernel_tap * dilation, kernel_tap * dilation + width_cells, axis=2)
        total_sum = total_sum + jnp.einsum('oc,cmn->omn', kernel_taps[kernel_tap].astype(jnp.float32), window_cells.astype(jnp.float32), precision=lax.Precision.HIGHEST)
    return jax.nn.silu(total_sum + kernel_bias[:, None, None])

def surrogate_block(member_rows, lift_gain, lift_bias, conv_first, bias_first, conv_second, bias_second, readout):
    width_cells = member_rows.shape[1]
    channels = lift_gain.shape[0]
    first_layer = jnp.tanh(lift_gain[:, None, None] * member_rows[None] + lift_bias[:, None, None]).astype(jnp.bfloat16)
    padded_first = jnp.pad(first_layer, ((0, 0), (0, 0), (1, 1)))
    second_layer = dilated_conv(padded_first, conv_first, bias_first, 1, width_cells).astype(jnp.bfloat16)
    joined_layers = jnp.concatenate([first_layer, second_layer], axis=0)
    padded_joined = jnp.pad(joined_layers, ((0, 0), (0, 0), (2, 2)))
    third_layer = dilated_conv(padded_joined, conv_second, bias_second, 2, width_cells).astype(jnp.bfloat16)
    readout_wide = readout.astype(jnp.float32)
    result = jnp.einsum('c,cmn->mn', readout_wide[:channels], first_layer.astype(jnp.float32), precision=lax.Precision.HIGHEST)
    result = result + jnp.einsum('c,cmn->mn', readout_wide[channels:2 * channels], second_layer.astype(jnp.float32), precision=lax.Precision.HIGHEST)
    result = result + jnp.einsum('c,cmn->mn', readout_wide[2 * channels:], third_layer.astype(jnp.float32), precision=lax.Precision.HIGHEST)
    return result

def surrogate(log_values, lift_gain, lift_bias, conv_first, bias_first, conv_second, bias_second, readout):
    blocks = log_values.reshape(MEMBERS // 16, 16, CELLS)

    def one_block(block_rows):
        return surrogate_block(block_rows, lift_gain, lift_bias, conv_first, bias_first, conv_second, bias_second, readout)
    return lax.map(one_block, blocks).reshape(MEMBERS, CELLS)

def gram_terms(neighbour_rows, innov_rows, obs_weight):
    anomaly = neighbour_rows - lax.optimization_barrier(jnp.mean(neighbour_rows, axis=1, keepdims=True))
    scaled = anomaly * obs_weight
    gram = jnp.einsum('bko,blo->bkl', scaled, anomaly, precision=lax.Precision.HIGHEST)
    rhs = jnp.einsum('bko,bo->bk', scaled, innov_rows, precision=lax.Precision.HIGHEST)
    return (gram, rhs)

def solve_weights(gram, rhs):
    order = gram.shape[-1]
    system = gram + (order - 1.0) * jnp.eye(order, dtype=gram.dtype)
    factor = jnp.linalg.cholesky(system)
    half_solved = jax.scipy.linalg.solve_triangular(factor, rhs[..., None], lower=True)
    solved = jax.scipy.linalg.solve_triangular(factor, half_solved, lower=True, trans=1)[..., 0]
    return solved - lax.optimization_barrier(jnp.mean(solved, axis=-1, keepdims=True))

def reference(log_field, obs_heads, obs_var, obs_noise, obs_index, obs_count, neighbours, lift_gain, lift_bias, conv_first, bias_first, conv_second, bias_second, readout):
    heads = surrogate(log_field, lift_gain, lift_bias, conv_first, bias_first, conv_second, bias_second, readout)
    tile_start = (jnp.arange(N_SPACE, dtype=jnp.int32) * CELLS_DEV)[:, None]
    cell_ids = (obs_index.astype(jnp.int32) + tile_start).reshape(-1)
    predicted = jnp.take(heads, cell_ids, axis=1)
    live_slots = (jnp.arange(OBS_CAP, dtype=jnp.int32)[None, :] < obs_count.astype(jnp.int32)[:, None]).reshape(-1)
    obs_weight = jnp.where(live_slots, 1.0 / obs_var, jnp.zeros_like(obs_var))
    innovation = obs_heads[None, :] + jnp.sqrt(obs_var)[None, :] * obs_noise - predicted

    def block_solve(block_args):
        member_ids, innov_rows = block_args
        gram, rhs = gram_terms(jnp.take(predicted, member_ids, axis=0), innov_rows, obs_weight)
        return solve_weights(gram, rhs)
    coef = lax.map(block_solve, (neighbours.reshape(MEMBERS // 16, 16, NEIGHBOURS), innovation.reshape(MEMBERS // 16, 16, OBS_TOTAL))).reshape(MEMBERS, NEIGHBOURS)
    row_ids = jnp.arange(MEMBERS, dtype=jnp.int32)[:, None]
    mixing = jnp.zeros((MEMBERS, MEMBERS), log_field.dtype).at[row_ids, neighbours.astype(jnp.int32)].add(coef)
    updated_field = log_field + jnp.dot(mixing, log_field, precision=lax.Precision.HIGHEST)
    new_heads = surrogate(updated_field, lift_gain, lift_bias, conv_first, bias_first, conv_second, bias_second, readout)
    return (updated_field, new_heads)
```

```python
import jax
import jax.numpy as jnp
from jax import lax
from jax.experimental import pallas as pl
from jax.experimental.pallas import tpu as pltpu
from jax.sharding import PartitionSpec as P

F32, BF16, I32 = jnp.float32, jnp.bfloat16, jnp.int32
HIGH = lax.Precision.HIGHEST
NY = 4
STEP = 4


def lanes(shape):
    return lax.broadcasted_iota(I32, shape, len(shape) - 1)


def rows(shape):
    return lax.broadcasted_iota(I32, shape, len(shape) - 2)


def column(row, count, offset=0):
    shape = (count, row.shape[1])
    picked = jnp.where(lanes(shape) == rows(shape) + offset, jnp.broadcast_to(row, shape), 0.0)
    return jnp.sum(picked, axis=1, keepdims=True)


def silu(value):
    half = 0.5 * value
    return half + half * jnp.tanh(half)


def exact_dot(left, right):
    return jnp.dot(left, right, precision=HIGH, preferred_element_type=F32)


def dot(left, right):
    return jnp.dot(left, right, preferred_element_type=F32)


def split3(value):
    top = value.astype(BF16)
    rest = value - top.astype(F32)
    middle = rest.astype(BF16)
    return top, middle, (rest - middle.astype(F32)).astype(BF16)


def kernel(
    sizes,
    fld, oheads, ovar, onoise, oindex, ocount, nbrs, gain, bias, conv1, bias1, conv2, bias2, rout,
    upd_out, head_out,
    const, wcentre, square, tall, fx, joined, ht,
    halo_l, halo_r, field_all, halo_all, nbr_all, onehot_col, onehot_row, own_hot,
    obs_cols, noise_t, panel, tiles, recv_y, part_z, recv_z, gram_rows, mix_rows, picks, recv_m,
    s_halo, r_halo, s_fld, r_fld, s_fh, r_fh, s_nb, r_nb, s_pan, r_pan, s_y, r_y, s_z, r_z,
    s_gz, r_gz, s_gy, r_gy, s_a, r_a, s_mz, r_mz, s_my, r_my,
):
    ns, nm, nz = sizes
    nq = nm // 2
    members = fld.shape[0]
    slots = ovar.shape[1]
    ch = gain.shape[1]
    s, m = lax.axis_index("space"), lax.axis_index("members")
    z, y = s // NY, lax.rem(s, NY)

    def copy(src, dst, send, recv, to_s, to_m):
        return pltpu.make_async_remote_copy(
            src_ref=src, dst_ref=dst, send_sem=send, recv_sem=recv,
            device_id={"space": to_s, "members": to_m}, device_id_type=pl.DeviceIdType.MESH,
        )

    def at_z(i):
        return lax.rem(z + i, nz)

    def at_y(i):
        return lax.rem(y + i, NY)

    def at_m(i):
        return lax.rem(m + i, nm)

    def each(count, action):
        def body(i, carry):
            action(i)
            return carry

        lax.fori_loop(1, count, body, 0)

    gate = pltpu.get_barrier_semaphore()

    def greet(to_s, to_m):
        pl.semaphore_signal(
            gate, inc=1, device_id={"space": to_s, "members": to_m},
            device_id_type=pl.DeviceIdType.MESH,
        )

    right, left = lax.rem(s + 1, ns), lax.rem(s + ns - 1, ns)
    greet(right, m)
    greet(left, m)
    each(nz, lambda i: greet(at_z(i) * NY + y, m))
    each(NY, lambda i: greet(z * NY + at_y(i), m))
    each(nm, lambda i: greet(s, at_m(i)))

    wide = (ch, 128)
    const[0] = jnp.broadcast_to(column(gain[...], ch), wide)
    const[1] = jnp.broadcast_to(column(bias[...], ch), wide)
    const[2] = jnp.broadcast_to(column(bias1[...], ch), wide)
    const[3] = jnp.broadcast_to(column(bias2[...], ch), wide)
    read = rout[...].astype(F32)
    const[4] = jnp.broadcast_to(column(read, ch, 2 * ch), wide)
    wcentre[0:ch, :] = conv2[1]
    wcentre[ch : ch + 16, :] = jnp.broadcast_to(read[:, 0 : 2 * ch], (16, 2 * ch)).astype(BF16)

    own_row = nbrs[pl.ds(s, 1), :]
    nbr_all[m] = jnp.zeros((8, 128), I32)
    nbr_all[m, :, 0:members] = jnp.broadcast_to(own_row, (8, members))
    field_all[m] = fld[...]

    variance = ovar[...]
    live = lanes((1, slots)) < ocount[0, 0]
    weight = jnp.where(live, 1.0 / variance, 0.0)
    obs_cols[0] = jnp.broadcast_to(column(weight, slots), (slots, 128))
    obs_cols[1] = jnp.broadcast_to(column(oheads[...], slots), (slots, 128))
    spread = jnp.broadcast_to(column(jnp.sqrt(variance), slots), (slots, 128))
    square[...] = jnp.zeros((128, 128), F32)
    square[0:members, 0:slots] = onoise[...]
    square[members : 2 * members, 0:slots] = onoise[...]
    noise_t[...] = square[...].T[0:slots, :] * spread
    cell = column(oindex[...].astype(F32), slots).astype(I32)

    half = members
    low = lanes((members, 128)) < half

    pl.semaphore_wait(gate, 2 + (nz - 1) + (NY - 1) + (nm - 1))

    to_right = copy(fld, halo_l, s_halo.at[0], r_halo.at[0], right, m)
    to_left = copy(fld, halo_r, s_halo.at[1], r_halo.at[1], left, m)
    to_right.start()
    to_left.start()

    def nbr_copy(i):
        return copy(nbr_all.at[m], nbr_all.at[m], s_nb.at[i], r_nb.at[i], s, at_m(i))

    def field_copy(i):
        return copy(field_all.at[m], field_all.at[m], s_fld.at[i], r_fld.at[i], s, at_m(i))

    def halo_copy(i):
        return copy(halo_all.at[m], halo_all.at[m], s_fh.at[i], r_fh.at[i], s, at_m(i))

    def build_fx(own, halos):
        square[0:members, :] = own
        square[members : 2 * members, :] = own
        tall[8:136, :] = square[...].T
        square[0:members, :] = halos
        square[members : 2 * members, :] = halos
        turned = square[...].T
        tall[0:8, :] = turned[0:8, :]
        tall[136:144, :] = turned[8:16, :]
        fx[0:70, :] = jnp.where(lanes((70, 128)) < half, tall[5:75, :], tall[69:139, :])

    def at(index):
        return pl.multiple_of(index * 128, 128)

    low_row = lanes((1, 128)) < half
    keep_l = jnp.where(jnp.logical_and(low_row, s == 0), 0.0, 1.0)
    keep_r = jnp.where(jnp.logical_and(jnp.logical_not(low_row), s == ns - 1), 0.0, 1.0)

    def surrogate():
        def lift(block, carry):
            for inner in range(10):
                index = block * 10 + inner
                value = jnp.tanh(const[0] * fx[pl.ds(index, 1), :] + const[1])
                joined[0:ch, pl.ds(at(index), 128)] = value.astype(BF16)
            return carry

        lax.fori_loop(0, 7, lift, 0)

        def mask(top, index, keep):
            where = (slice(top, top + ch), slice(index * 128, index * 128 + 128))
            joined[where] = (joined[where].astype(F32) * keep).astype(BF16)

        for index in (0, 1, 2):
            mask(0, index, keep_l)
        for index in (67, 68, 69):
            mask(0, index, keep_r)

        size = STEP * 128
        b1 = const[2][:, 0:1]
        b2 = const[3][:, 0:1]
        ro3 = const[4][:, 0:1]

        def middle(block, carry):
            base = block * STEP
            total = dot(conv1[0], joined[0:ch, pl.ds(at(base), size)])
            total += dot(conv1[1], joined[0:ch, pl.ds(at(base + 1), size)])
            total += dot(conv1[2], joined[0:ch, pl.ds(at(base + 2), size)])
            joined[ch : 2 * ch, pl.ds(at(base + 1), size)] = silu(total + b1).astype(BF16)
            return carry

        lax.fori_loop(0, 68 // STEP, middle, 0)
        for index in (1, 2):
            mask(ch, index, keep_l)
        for index in (67, 68):
            mask(ch, index, keep_r)

        def last(block, carry):
            base = block * STEP
            centre = dot(wcentre[...], joined[:, pl.ds(at(base + 3), size)])
            total = centre[0:ch]
            total += dot(conv2[0], joined[:, pl.ds(at(base + 1), size)])
            total += dot(conv2[2], joined[:, pl.ds(at(base + 5), size)])
            third = silu(total + b2).astype(BF16).astype(F32)
            head = centre[ch : ch + 1] + jnp.sum(third * ro3, axis=0, keepdims=True)
            for inner in range(STEP):
                ht[pl.ds(base + inner, 1), :] = head[:, inner * 128 : inner * 128 + 128]
            return carry

        lax.fori_loop(0, 64 // STEP, last, 0)

    to_right.wait()
    to_left.wait()
    wide_lane = lanes((members, 128))
    halo_all[m] = jnp.where(
        wide_lane < 8,
        pltpu.roll(halo_l[...], 8, 1),
        jnp.where(wide_lane < 16, pltpu.roll(halo_r[...], 8, 1), 0.0),
    )
    each(nm, lambda i: nbr_copy(i).start())
    each(nm, lambda i: field_copy(i).start())
    each(nm, lambda i: halo_copy(i).start())

    build_fx(fld[...], halo_all[m])
    surrogate()

    narrow = (slots, 64)
    first_half = (lanes(narrow) == cell).astype(F32)
    second_half = (lanes(narrow) + 64 == cell).astype(F32)
    heads_t = ht[...]
    wide_obs = lanes((slots, 128))
    both = jnp.where(wide_obs < half, exact_dot(first_half, heads_t), exact_dot(second_half, heads_t))
    own_pred = both + pltpu.roll(both, half, 1)
    panel[m] = own_pred

    def panel_copy(i):
        return copy(panel.at[m], panel.at[m], s_pan.at[i], r_pan.at[i], s, at_m(i))

    each(nm, lambda i: panel_copy(i).start())

    each(nm, lambda i: nbr_copy(i).wait())
    for pair in range(nq):
        lane_ids = jnp.where(
            lanes((1, 128)) < half,
            nbr_all[2 * pair, 0:1, :],
            pltpu.roll(nbr_all[2 * pair + 1], half, 1)[0:1, :],
        )
        grid = (nm * members, 128)
        onehot_col[:, pair * 128 : pair * 128 + 128] = (rows(grid) == lane_ids).astype(F32).astype(BF16)
        ids = column(lane_ids.astype(F32), 128).astype(I32)
        fold = (128, 3 * members)
        onehot_row[pair * 128 : pair * 128 + 128, :] = (
            (jnp.bitwise_and(lanes(fold), members - 1) + m * members == ids).astype(F32).astype(BF16)
        )
    own_ids = column(own_row.astype(F32), members).astype(I32)
    own_hot[...] = (lanes((members, nm * members)) == own_ids).astype(F32)

    each(nm, lambda i: panel_copy(i).wait())
    pairs = [jnp.where(wide_obs < half, panel[2 * q], panel[2 * q + 1]) for q in range(nq)]
    total = pairs[0]
    for q in range(1, nq):
        total = total + pairs[q]
    centre = jnp.sum(total, axis=1, keepdims=True) / (nm * members)
    innovation = obs_cols[1] + noise_t[...] - own_pred
    lead = (obs_cols[0] * jnp.where(wide_obs < half, own_pred - centre, innovation)).T
    for q in range(nq):
        block = exact_dot(lead, pairs[q] - centre)
        tiles[:, :, q, :] = block[0:members].reshape(nz, NY, 128)
        tiles[:, :, nq + q, :] = block[members : 2 * members].reshape(nz, NY, 128)

    def y_copy(i):
        return copy(tiles.at[:, at_y(i)], recv_y.at[i], s_y.at[i], r_y.at[i], z * NY + at_y(i), m)

    each(NY, lambda i: y_copy(i).start())
    each(NY, lambda i: y_copy(i).wait())
    part_z[...] = (tiles[:, y] + recv_y[1]) + (recv_y[2] + recv_y[3])

    def z_copy(i):
        return copy(part_z.at[at_z(i)], recv_z.at[i], s_z.at[i], r_z.at[i], at_z(i) * NY + y, m)

    each(nz, lambda i: z_copy(i).start())
    each(nz, lambda i: z_copy(i).wait())
    own_tile = part_z[z]
    for i in range(1, nz):
        own_tile = own_tile + recv_z[i]

    def gather_rows(buffer, sz, rz, sy, ry):
        def by_z(i):
            return copy(buffer.at[z, y], buffer.at[z, y], sz.at[i], rz.at[i], at_z(i) * NY + y, m)

        def by_y(i):
            return copy(buffer.at[:, y], buffer.at[:, y], sy.at[i], ry.at[i], z * NY + at_y(i), m)

        each(nz, lambda i: by_z(i).start())
        each(nz, lambda i: by_z(i).wait())
        each(NY, lambda i: by_y(i).start())
        each(NY, lambda i: by_y(i).wait())

    gram_rows[z, y] = own_tile[0:nq]
    gather_rows(gram_rows, s_gz, r_gz, s_gy, r_gy)

    parts = [split3(gram_rows[:, :, q, :].reshape(members, 128)) for q in range(nq)]
    stacked = jnp.concatenate(
        [jnp.concatenate([parts[q][k] for q in range(nq)], axis=1) for k in range(3)], axis=0
    )
    chosen = dot(stacked, onehot_col[...])
    chosen = chosen[0:members] + (chosen[members : 2 * members] + chosen[2 * members : 3 * members])
    for pair in range(nq):
        lump = jnp.concatenate(split3(chosen[:, pair * 128 : pair * 128 + 128]), axis=0)
        picked = dot(onehot_row[pair * 128 : pair * 128 + 128, :], lump)
        picks[2 * pair] = picked[0:members]
        picks[2 * pair + 1] = picked[members : 2 * members]

    def pick_copy(i):
        return copy(picks.at[at_m(i)], recv_m.at[i], s_a.at[i], r_a.at[i], s, at_m(i))

    each(nm, lambda i: pick_copy(i).start())
    rhs = jnp.zeros((members, 1), F32)
    for q in range(nq):
        line = jnp.broadcast_to(own_tile[nq + q : nq + q + 1], (members, 128))
        rhs = rhs + jnp.sum(line * own_hot[:, q * 128 : q * 128 + 128], axis=1, keepdims=True)
    rhs = rhs - jnp.mean(rhs, axis=0, keepdims=True)
    each(nm, lambda i: pick_copy(i).wait())
    gram = picks[m]
    for i in range(1, nm):
        gram = gram + recv_m[i]
    gram = jnp.where(lax.rem(m, 2) == 1, pltpu.roll(gram, half, 1), gram)
    gram = jnp.where(low, gram, 0.0)
    row_mean = jnp.sum(gram, axis=1, keepdims=True) / members
    col_mean = jnp.sum(gram, axis=0, keepdims=True) / members
    all_mean = jnp.sum(row_mean, axis=0, keepdims=True) / members
    gram = jnp.where(low, gram - row_mean - col_mean + all_mean, 0.0)
    row_ids = rows((members, 128))
    gram = gram + jnp.where(wide_lane == row_ids, members - 1.0, 0.0)
    gram = jnp.where(wide_lane == members, rhs, gram)

    def eliminate(step, system):
        for p in range(0, 8, 2):
            row0, row1 = system[p : p + 1], system[p + 1 : p + 2]
            col0, col1 = system[:, p : p + 1], system[:, p + 1 : p + 2]
            a, b = col0[p : p + 1], col1[p : p + 1]
            c, d = col0[p + 1 : p + 2], col1[p + 1 : p + 2]
            inverse = 1.0 / (a * d - b * c)
            new0 = (d * row0 - b * row1) * inverse
            new1 = (a * row1 - c * row0) * inverse
            rest = system - col0 * new0 - col1 * new1
            system = jnp.where(row_ids == p, new0, jnp.where(row_ids == p + 1, new1, rest))
        system = jnp.concatenate([system[8:], system[0:8]], axis=0)
        return pltpu.roll(system, 120, 1)

    solved = lax.fori_loop(0, members // 8, eliminate, gram)[:, 0:1]
    coef = solved - jnp.mean(solved, axis=0, keepdims=True)
    mix = jnp.sum(own_hot[...] * coef, axis=0, keepdims=True)
    for q in range(nq):
        mix_rows[z, y, q : q + 1] = mix[:, q * 128 : q * 128 + 128]
    gather_rows(mix_rows, s_mz, r_mz, s_my, r_my)

    each(nm, lambda i: field_copy(i).wait())
    each(nm, lambda i: halo_copy(i).wait())
    updated = fld[...]
    halos = halo_all[m]
    for q in range(nq):
        part = mix_rows[:, :, q, :].reshape(members, 128)
        updated = updated + exact_dot(part, field_all[2 * q : 2 * q + 2].reshape(128, 128))
        halos = halos + exact_dot(part, halo_all[2 * q : 2 * q + 2].reshape(128, 128))
    upd_out[...] = updated
    build_fx(updated, halos)
    surrogate()
    square[0:members, :] = ht[...]
    square[members : 2 * members, :] = ht[...]
    turned = square[...].T
    head_out[...] = jnp.where(low, turned[0:members], turned[members : 2 * members])


def solution(mesh):
    ns, nm = mesh.shape["space"], mesh.shape["members"]
    nz, nq = ns // NY, nm // 2
    dma = pltpu.SemaphoreType.DMA
    vmem = pltpu.VMEM

    def on_device(
        log_field, obs_heads, obs_var, obs_noise, obs_index, obs_count, neighbours,
        lift_gain, lift_bias, conv_first, bias_first, conv_second, bias_second, readout,
    ):
        members, cells = log_field.shape
        slots = obs_var.shape[0]
        ch = lift_gain.shape[0]
        block = (members, 128)
        out = jax.ShapeDtypeStruct((members, cells), F32)
        in_vmem = pl.BlockSpec(memory_space=pltpu.VMEM)
        specs = [in_vmem] * 14
        specs[5] = pl.BlockSpec(memory_space=pltpu.SMEM)
        scratch = [
            vmem((5, ch, 128), F32), vmem((ch + 16, 2 * ch), BF16), vmem((128, 128), F32),
            vmem((144, 128), F32), vmem((72, 128), F32), vmem((2 * ch, 70 * 128), BF16),
            vmem((64, 128), F32),
            vmem(block, F32), vmem(block, F32), vmem((nm, *block), F32), vmem((nm, *block), F32),
            vmem((nm, 8, 128), I32), vmem((nm * members, nm * members), BF16),
            vmem((nm * members, 3 * members), BF16), vmem((members, nm * members), F32),
            vmem((2, slots, 128), F32), vmem((slots, 128), F32), vmem((nm, slots, 128), F32),
            vmem((nz, NY, nm, 128), F32), vmem((NY, nz, nm, 128), F32), vmem((nz, nm, 128), F32),
            vmem((nz, nm, 128), F32), vmem((nz, NY, nq, 128), F32), vmem((nz, NY, nq, 128), F32),
            vmem((nm, *block), F32), vmem((nm, *block), F32),
            dma((2,)), dma((2,)),
            *[dma((nm,))] * 8,
            dma((NY,)), dma((NY,)), dma((nz,)), dma((nz,)),
            dma((nz,)), dma((nz,)), dma((NY,)), dma((NY,)),
            dma((nm,)), dma((nm,)),
            dma((nz,)), dma((nz,)), dma((NY,)), dma((NY,)),
        ]

        def body(*refs):
            kernel((ns, nm, nz), *refs)

        return pl.pallas_call(
            body,
            out_shape=(out, out),
            in_specs=specs,
            out_specs=(in_vmem, in_vmem),
            scratch_shapes=scratch,
            name="smoother",
            compiler_params=pltpu.CompilerParams(
                collective_id=0, has_side_effects=True, vmem_limit_bytes=40 * 1024 * 1024
            ),
        )(
            log_field, obs_heads[None], obs_var[None], obs_noise, obs_index, obs_count[None],
            neighbours, lift_gain[None], lift_bias[None], conv_first, bias_first[None],
            conv_second, bias_second[None], readout[None],
        )

    in_specs = (
        P("members", "space"), P("space"), P("space"), P("members", "space"), P("space", None),
        P("space"), P("members", None), P(), P(), P(), P(), P(), P(), P(),
    )
    out_specs = (P("members", "space"), P("members", "space"))
    return jax.shard_map(
        on_device, mesh=mesh, in_specs=in_specs, out_specs=out_specs, check_vma=False
    )
```

```python
import jax
import jax.numpy as jnp
from jax import lax
from jax.experimental import pallas as pl
from jax.experimental.pallas import tpu as pltpu
from jax.sharding import PartitionSpec as P

F32, BF16, I32 = jnp.float32, jnp.bfloat16, jnp.int32
HIGH = lax.Precision.HIGHEST
NY = 4
STEP = 4
PIVOTS = 8


def lanes(shape):
    return lax.broadcasted_iota(I32, shape, len(shape) - 1)


def rows(shape):
    return lax.broadcasted_iota(I32, shape, len(shape) - 2)


def column(row, count, offset=0):
    shape = (count, row.shape[1])
    picked = jnp.where(lanes(shape) == rows(shape) + offset, jnp.broadcast_to(row, shape), 0.0)
    return jnp.sum(picked, axis=1, keepdims=True)


def silu(value):
    half = 0.5 * value
    return half + half * jnp.tanh(half)


def exact_dot(left, right):
    return jnp.dot(left, right, precision=HIGH, preferred_element_type=F32)


def dot(left, right):
    return jnp.dot(left, right, preferred_element_type=F32)


def split3(value):
    top = value.astype(BF16)
    rest = value - top.astype(F32)
    middle = rest.astype(BF16)
    return top, middle, (rest - middle.astype(F32)).astype(BF16)


def eliminate(step, system):
    sub = rows((PIVOTS, 128))

    def spread(block, k):
        return jnp.broadcast_to(block[k : k + 1], (PIVOTS, 128))

    columns = [jnp.broadcast_to(system[:, k : k + 1], system.shape) for k in range(PIVOTS)]
    corner = [column_k[0:PIVOTS] for column_k in columns]
    lines = system[0:PIVOTS]
    for k in range(PIVOTS):
        inverse = 1.0 / spread(corner[k], k)
        here = sub == k
        line = spread(lines, k) * inverse
        lines = jnp.where(here, line, lines - corner[k] * line)
        for j in range(k + 1, PIVOTS):
            entry = spread(corner[j], k) * inverse
            corner[j] = jnp.where(here, entry, corner[j] - corner[k] * entry)
    rest = system[PIVOTS:]
    for k in range(PIVOTS):
        rest = rest - columns[k][PIVOTS:] * lines[k : k + 1]
    return pltpu.roll(jnp.concatenate([rest, lines], axis=0), 128 - PIVOTS, 1)


def kernel(
    sizes,
    h_fld, h_oheads, h_ovar, h_noise, h_oindex, h_ocount, h_nbrs, h_gain, h_bias, h_conv1, h_bias1,
    h_conv2, h_bias2, h_rout,
    upd_out, head_out,
    oheads, ovar, noise, oindex, ocount, nbrs, gain, bias, conv1, bias1, conv2, bias2, rout,
    const, wcentre, square, tall, fx, joined, ht,
    halo_l, halo_r, field_all, halo_all, nbr_all, onehot_col, onehot_row, own_hot,
    obs_all, panel, tiles, recv_z, gram_rows, mix_rows, picks, recv_m,
    s_in, s_halo, r_halo, s_fld, r_fld, s_fh, r_fh, s_nb, r_nb, s_a, r_a, s_pan, r_pan,
    s_ob, r_ob, s_z, r_z, s_gz, r_gz, s_gy, r_gy, s_mz, r_mz, s_my, r_my,
):
    ns, nm, nz = sizes
    nq = nm // 2
    members = nbrs.shape[0]
    slots = ovar.shape[1]
    ch = gain.shape[1]
    half = members
    s, m = lax.axis_index("space"), lax.axis_index("members")
    z, y = s // NY, lax.rem(s, NY)
    own = y * nz + z

    def copy(src, dst, send, recv, to_s, to_m):
        return pltpu.make_async_remote_copy(
            src_ref=src, dst_ref=dst, send_sem=send, recv_sem=recv,
            device_id={"space": to_s, "members": to_m}, device_id_type=pl.DeviceIdType.MESH,
        )

    def at_z(i):
        return lax.rem(z + i, nz)

    def at_y(i):
        return lax.rem(y + i, NY)

    def at_m(i):
        return lax.rem(m + i, nm)

    def each(count, action):
        def body(i, carry):
            action(i)
            return carry

        lax.fori_loop(1, count, body, 0)

    def each_far(action):
        def body(t, carry):
            action(nz // 2 + (t + 1) // 2 * (2 * lax.rem(t, 2) - 1))
            return carry

        lax.fori_loop(0, nz - 1, body, 0)

    def each_ym(action):
        def body(i, carry):
            action(i // nm, lax.rem(i, nm))
            return carry

        lax.fori_loop(1, NY * nm, body, 0)

    loads = [
        pltpu.make_async_copy(src, dst, s_in.at[k])
        for k, (src, dst) in enumerate([
            (h_fld, field_all.at[m]), (h_gain, gain), (h_bias, bias), (h_bias1, bias1),
            (h_bias2, bias2), (h_rout, rout), (h_conv1, conv1), (h_conv2, conv2), (h_nbrs, nbrs),
            (h_ovar, ovar), (h_oheads, oheads), (h_ocount, ocount), (h_noise, noise),
            (h_oindex, oindex),
        ])
    ]
    for load in loads:
        load.start()

    gate = pltpu.get_barrier_semaphore()

    def greet(to_s, to_m):
        pl.semaphore_signal(
            gate, inc=1, device_id={"space": to_s, "members": to_m},
            device_id_type=pl.DeviceIdType.MESH,
        )

    right, left = lax.rem(s + 1, ns), lax.rem(s + ns - 1, ns)
    each_far(lambda i: greet(at_z(i) * NY + y, m))
    greet(right, m)
    greet(left, m)
    each_ym(lambda i, j: greet(z * NY + at_y(i), at_m(j)))
    for load in loads:
        load.wait()
    own_row = nbrs[pl.ds(own, 1), :]
    nbr_all[m] = jnp.zeros((8, 128), I32)
    nbr_all[m, :, 0:members] = jnp.broadcast_to(own_row, (8, members))
    pl.semaphore_wait(gate, 2 + (nz - 1) + (NY * nm - 1))

    fld = field_all.at[m]
    to_right = copy(fld, halo_l, s_halo.at[0], r_halo.at[0], right, m)
    to_left = copy(fld, halo_r, s_halo.at[1], r_halo.at[1], left, m)
    to_right.start()
    to_left.start()

    def nbr_copy(i):
        return copy(nbr_all.at[m], nbr_all.at[m], s_nb.at[i], r_nb.at[i], s, at_m(i))

    def field_copy(i):
        return copy(field_all.at[m], field_all.at[m], s_fld.at[i], r_fld.at[i], s, at_m(i))

    def halo_copy(i):
        return copy(halo_all.at[m], halo_all.at[m], s_fh.at[i], r_fh.at[i], s, at_m(i))

    each(nm, lambda i: nbr_copy(i).start())
    each(nm, lambda i: field_copy(i).start())

    wide = (ch, 128)
    const[0] = jnp.broadcast_to(column(gain[...], ch), wide)
    const[1] = jnp.broadcast_to(column(bias[...], ch), wide)
    const[2] = jnp.broadcast_to(column(bias1[...], ch), wide)
    const[3] = jnp.broadcast_to(column(bias2[...], ch), wide)
    read = rout[...].astype(F32).reshape(1, 3 * ch)
    const[4] = jnp.broadcast_to(column(read, ch, 2 * ch), wide)
    wcentre[0:ch, :] = conv2[1]
    wcentre[ch : ch + 16, :] = jnp.broadcast_to(read[:, 0 : 2 * ch], (16, 2 * ch)).astype(BF16)

    low = lanes((members, 128)) < half
    wide_lane = lanes((members, 128))
    low_row = lanes((1, 128)) < half
    keep_l = jnp.where(jnp.logical_and(low_row, s == 0), 0.0, 1.0)
    keep_r = jnp.where(jnp.logical_and(jnp.logical_not(low_row), s == ns - 1), 0.0, 1.0)

    def at(index):
        return pl.multiple_of(index * 128, 128)

    def lift_row(index):
        value = jnp.tanh(const[0] * fx[pl.ds(index + 5, 1), :] + const[1])
        joined[0:ch, pl.ds(at(index), 128)] = value.astype(BF16)

    def mask(top, index, keep):
        where = (slice(top, top + ch), slice(index * 128, index * 128 + 128))
        joined[where] = (joined[where].astype(F32) * keep).astype(BF16)

    def lift_inner(values):
        square[0:members, :] = values
        square[members : 2 * members, :] = values
        tall[8:136, :] = square[...].T
        fx[8:72, :] = jnp.where(lanes((64, 128)) < half, tall[8:72, :], tall[72:136, :])

        def block(k, carry):
            for inner in range(8):
                lift_row(3 + k * 8 + inner)
            return carry

        lax.fori_loop(0, 8, block, 0)

    def lift_outer(halos):
        square[0:members, :] = halos
        square[members : 2 * members, :] = halos
        turned = square[...].T
        near = lanes((8, 128)) < half
        fx[0:8, :] = jnp.where(near, turned[0:8, :], tall[64:72, :])
        fx[72:80, :] = jnp.where(near, tall[72:80, :], turned[8:16, :])
        for index in (0, 1, 2):
            lift_row(index)
            mask(0, index, keep_l)
        for index in (67, 68, 69):
            lift_row(index)
            mask(0, index, keep_r)

    def convolve():
        size = STEP * 128
        b1 = const[2][:, 0:1]
        b2 = const[3][:, 0:1]
        ro3 = const[4][:, 0:1]

        def middle(block, carry):
            base = block * STEP
            total = dot(conv1[0], joined[0:ch, pl.ds(at(base), size)])
            total += dot(conv1[1], joined[0:ch, pl.ds(at(base + 1), size)])
            total += dot(conv1[2], joined[0:ch, pl.ds(at(base + 2), size)])
            joined[ch : 2 * ch, pl.ds(at(base + 1), size)] = silu(total + b1).astype(BF16)
            return carry

        lax.fori_loop(0, 68 // STEP, middle, 0, unroll=68 // STEP)
        for index in (1, 2):
            mask(ch, index, keep_l)
        for index in (67, 68):
            mask(ch, index, keep_r)

        def last(block, carry):
            base = block * STEP
            centre = dot(wcentre[...], joined[:, pl.ds(at(base + 3), size)])
            total = centre[0:ch]
            total += dot(conv2[0], joined[:, pl.ds(at(base + 1), size)])
            total += dot(conv2[2], joined[:, pl.ds(at(base + 5), size)])
            third = silu(total + b2).astype(BF16).astype(F32)
            head = centre[ch : ch + 1] + jnp.sum(third * ro3, axis=0, keepdims=True)
            for inner in range(STEP):
                ht[pl.ds(base + inner, 1), :] = head[:, inner * 128 : inner * 128 + 128]
            return carry

        lax.fori_loop(0, 64 // STEP, last, 0, unroll=64 // STEP)

    lift_inner(fld[...])

    to_right.wait()
    to_left.wait()
    halo_all[m] = jnp.where(
        wide_lane < 8,
        pltpu.roll(halo_l[...], 8, 1),
        jnp.where(wide_lane < 16, pltpu.roll(halo_r[...], 8, 1), 0.0),
    )
    each(nm, lambda i: halo_copy(i).start())
    lift_outer(halo_all[m])
    convolve()

    cell = column(oindex[...].astype(F32), slots).astype(I32)
    narrow = (slots, 64)
    first_half = (lanes(narrow) == cell).astype(F32)
    second_half = (lanes(narrow) + 64 == cell).astype(F32)
    heads_t = ht[...]
    wide_obs = lanes((slots, 128))
    both = jnp.where(wide_obs < half, exact_dot(first_half, heads_t), exact_dot(second_half, heads_t))
    panel[y, m] = both + pltpu.roll(both, half, 1)

    def panel_copy(i, j):
        k = i * nm + j
        here = panel.at[y, m]
        return copy(here, here, s_pan.at[k], r_pan.at[k], z * NY + at_y(i), at_m(j))

    each_ym(lambda i, j: panel_copy(i, j).start())

    variance = ovar[...]
    live = lanes((1, slots)) < ocount[0]
    weight = jnp.where(live, 1.0 / variance, 0.0)
    tile_t = noise[...] * column(jnp.sqrt(variance), slots) + column(oheads[...], slots)
    obs_all[y, 0, :, 0:members] = tile_t
    obs_all[y, 0, :, members : 2 * members] = tile_t
    obs_all[y, 1] = jnp.broadcast_to(column(weight, slots), (slots, 128))

    def obs_copy(i):
        return copy(obs_all.at[y], obs_all.at[y], s_ob.at[i], r_ob.at[i], z * NY + at_y(i), m)

    each(NY, lambda i: obs_copy(i).start())
    own_ids = column(own_row.astype(F32), members).astype(I32)
    own_hot[...] = (lanes((members, nm * members)) == own_ids).astype(F32)
    each_ym(lambda i, j: panel_copy(i, j).wait())
    each(NY, lambda i: obs_copy(i).wait())

    depth = NY * slots
    deep = lanes((depth, 128)) < half
    pairs = [
        jnp.where(
            deep, panel[:, 2 * q].reshape(depth, 128), panel[:, 2 * q + 1].reshape(depth, 128)
        )
        for q in range(nq)
    ]
    total = pairs[0]
    for q in range(1, nq):
        total = total + pairs[q]
    centre = jnp.sum(total, axis=1, keepdims=True) / (nm * members)
    mine = panel[:, m].reshape(depth, 128)
    data = obs_all[:, 0].reshape(depth, 128)
    lead = obs_all[:, 1].reshape(depth, 128) * jnp.where(deep, mine - centre, data - mine)
    square[...] = lead.T
    first = pl.multiple_of(y * nz, nz)
    left_side = jnp.concatenate(
        [square[pl.ds(first, nz), :], square[pl.ds(members + first, nz), :]], axis=0
    )
    block = exact_dot(left_side, jnp.concatenate([pair - centre for pair in pairs], axis=1))
    for q in range(nq):
        tiles[:, q, :] = block[0:nz, q * 128 : q * 128 + 128]
        tiles[:, nq + q, :] = block[nz : 2 * nz, q * 128 : q * 128 + 128]

    def z_copy(i):
        return copy(tiles.at[at_z(i)], recv_z.at[i], s_z.at[i], r_z.at[i], at_z(i) * NY + y, m)

    each_far(lambda i: z_copy(i).start())

    each(nm, lambda i: nbr_copy(i).wait())
    for pair in range(nq):
        lane_ids = jnp.where(
            low_row, nbr_all[2 * pair, 0:1, :], pltpu.roll(nbr_all[2 * pair + 1], half, 1)[0:1, :]
        )
        grid = (nm * members, 128)
        onehot_col[:, pair * 128 : pair * 128 + 128] = (rows(grid) == lane_ids).astype(F32).astype(BF16)
        ids = column(lane_ids.astype(F32), 128).astype(I32)
        fold = (128, 3 * members)
        onehot_row[pair * 128 : pair * 128 + 128, :] = (
            (jnp.bitwise_and(lanes(fold), members - 1) + m * members == ids).astype(F32).astype(BF16)
        )

    each(nz, lambda i: z_copy(i).wait())
    own_tile = tiles[z]
    for i in range(1, nz):
        own_tile = own_tile + recv_z[i]

    def gather_rows(buffer, sz, rz, sy, ry, meanwhile):
        def by_z(i):
            here = buffer.at[y, z]
            return copy(here, here, sz.at[i], rz.at[i], at_z(i) * NY + y, m)

        def by_y(i):
            return copy(buffer.at[y], buffer.at[y], sy.at[i], ry.at[i], z * NY + at_y(i), m)

        each_far(lambda i: by_z(i).start())
        result = meanwhile()
        each(nz, lambda i: by_z(i).wait())
        each(NY, lambda i: by_y(i).start())
        each(NY, lambda i: by_y(i).wait())
        return result

    def right_side():
        value = jnp.zeros((members, 1), F32)
        for q in range(nq):
            line = jnp.broadcast_to(own_tile[nq + q : nq + q + 1], (members, 128))
            value = value + jnp.sum(line * own_hot[:, q * 128 : q * 128 + 128], axis=1, keepdims=True)
        return value - jnp.mean(value, axis=0, keepdims=True)

    gram_rows[y, z] = own_tile[0:nq]
    rhs = gather_rows(gram_rows, s_gz, r_gz, s_gy, r_gy, right_side)

    parts = [split3(gram_rows[:, :, q, :].reshape(members, 128)) for q in range(nq)]
    stacked = jnp.concatenate(
        [jnp.concatenate([parts[q][k] for q in range(nq)], axis=1) for k in range(3)], axis=0
    )
    chosen = dot(stacked, onehot_col[...])
    chosen = chosen[0:members] + (chosen[members : 2 * members] + chosen[2 * members : 3 * members])
    short = members // 2
    low_short = lanes((short, 128)) < half
    for pair in range(nq):
        lump = jnp.concatenate(split3(chosen[:, pair * 128 : pair * 128 + 128]), axis=0)
        picked = dot(onehot_row[pair * 128 : pair * 128 + 128, :], lump)
        turned = pltpu.roll(picked, half, 1)
        picks[2 * pair] = jnp.where(low_short, picked[0:short], turned[short:members])
        picks[2 * pair + 1] = jnp.where(
            low_short, turned[members : members + short], picked[members + short : 2 * members]
        )

    def pick_copy(i):
        return copy(picks.at[at_m(i)], recv_m.at[i], s_a.at[i], r_a.at[i], s, at_m(i))

    each(nm, lambda i: pick_copy(i).start())
    each(nm, lambda i: pick_copy(i).wait())
    packed = picks[m]
    for i in range(1, nm):
        packed = packed + recv_m[i]
    gram = jnp.concatenate([packed, pltpu.roll(packed, half, 1)], axis=0)
    gram = jnp.where(low, gram, 0.0)
    row_mean = jnp.sum(gram, axis=1, keepdims=True) / members
    col_mean = jnp.sum(gram, axis=0, keepdims=True) / members
    all_mean = jnp.sum(row_mean, axis=0, keepdims=True) / members
    gram = jnp.where(low, gram - row_mean - col_mean + all_mean, 0.0)
    gram = gram + jnp.where(wide_lane == rows((members, 128)), members - 1.0, 0.0)
    gram = jnp.where(wide_lane == members, rhs, gram)

    solved = lax.fori_loop(0, members // PIVOTS, eliminate, gram)[:, 0:1]
    coef = solved - jnp.mean(solved, axis=0, keepdims=True)
    mix = jnp.sum(own_hot[...] * coef, axis=0, keepdims=True)
    for q in range(nq):
        mix_rows[y, z, q : q + 1] = mix[:, q * 128 : q * 128 + 128]

    def arrivals():
        each(nm, lambda i: field_copy(i).wait())
        each(nm, lambda i: halo_copy(i).wait())

    gather_rows(mix_rows, s_mz, r_mz, s_my, r_my, arrivals)

    updated = fld[...]
    halos = halo_all[m]
    for q in range(nq):
        part = mix_rows[:, :, q, :].reshape(members, 128)
        updated = updated + exact_dot(part, field_all[2 * q : 2 * q + 2].reshape(128, 128))
        halos = halos + exact_dot(part, halo_all[2 * q : 2 * q + 2].reshape(128, 128))
    upd_out[...] = updated
    lift_inner(updated)
    lift_outer(halos)
    convolve()
    square[0:members, :] = ht[...]
    square[members : 2 * members, :] = ht[...]
    turned = square[...].T
    head_out[...] = jnp.where(low, turned[0:members], turned[members : 2 * members])


def solution(mesh):
    ns, nm = mesh.shape["space"], mesh.shape["members"]
    nz, nq = ns // NY, nm // 2
    dma = pltpu.SemaphoreType.DMA
    vmem = pltpu.VMEM

    def on_device(
        log_field, obs_heads, obs_var, obs_noise, obs_index, obs_count, neighbours,
        lift_gain, lift_bias, conv_first, bias_first, conv_second, bias_second, readout,
    ):
        members, cells = log_field.shape
        slots = obs_var.shape[0]
        ch = lift_gain.shape[0]
        block = (members, 128)
        out = jax.ShapeDtypeStruct((members, cells), F32)
        in_vmem = pl.BlockSpec(memory_space=pltpu.VMEM)
        in_place = pl.BlockSpec(memory_space=pltpu.HBM)
        given = (
            log_field, obs_heads[None], obs_var[None], obs_noise.T, obs_index, obs_count,
            neighbours, lift_gain[None], lift_bias[None], conv_first, bias_first[None],
            conv_second, bias_second[None], readout,
        )
        scratch = [
            *[
                (pltpu.SMEM if value.shape == (1,) else vmem)(value.shape, value.dtype)
                for value in given[1:]
            ],
            vmem((5, ch, 128), F32), vmem((ch + 16, 2 * ch), BF16), vmem((128, 128), F32),
            vmem((144, 128), F32), vmem((80, 128), F32), vmem((2 * ch, 70 * 128), BF16),
            vmem((64, 128), F32),
            vmem(block, F32), vmem(block, F32), vmem((nm, *block), F32), vmem((nm, *block), F32),
            vmem((nm, 8, 128), I32), vmem((nm * members, nm * members), BF16),
            vmem((nm * members, 3 * members), BF16), vmem((members, nm * members), F32),
            vmem((NY, 2, slots, 128), F32), vmem((NY, nm, slots, 128), F32),
            vmem((nz, nm, 128), F32), vmem((nz, nm, 128), F32),
            vmem((NY, nz, nq, 128), F32), vmem((NY, nz, nq, 128), F32),
            vmem((nm, members // 2, 128), F32), vmem((nm, members // 2, 128), F32),
            dma((len(given),)), dma((2,)), dma((2,)),
            *[dma((nm,))] * 8,
            dma((NY * nm,)), dma((NY * nm,)),
            dma((NY,)), dma((NY,)), dma((nz,)), dma((nz,)),
            dma((nz,)), dma((nz,)), dma((NY,)), dma((NY,)),
            dma((nz,)), dma((nz,)), dma((NY,)), dma((NY,)),
        ]

        def body(*refs):
            kernel((ns, nm, nz), *refs)

        return pl.pallas_call(
            body,
            out_shape=(out, out),
            in_specs=[in_place] * len(given),
            out_specs=(in_vmem, in_vmem),
            scratch_shapes=scratch,
            name="smoother",
            compiler_params=pltpu.CompilerParams(
                collective_id=0, has_side_effects=True, vmem_limit_bytes=32 * 1024 * 1024
            ),
        )(*given)

    in_specs = (
        P("members", "space"), P("space"), P("space"), P("members", "space"), P("space", None),
        P("space"), P("members", None), P(), P(), P(), P(), P(), P(), P(),
    )
    out_specs = (P("members", "space"), P("members", "space"))
    return jax.shard_map(
        on_device, mesh=mesh, in_specs=in_specs, out_specs=out_specs, check_vma=False
    )
```

```python
import jax
import jax.numpy as jnp
from jax import lax
from jax.experimental import pallas as pl
from jax.experimental.pallas import tpu as pltpu
from jax.sharding import PartitionSpec as P

F32, BF16, I32 = jnp.float32, jnp.bfloat16, jnp.int32
HIGH = lax.Precision.HIGHEST
NY = 4
STEP = 4
PIVOTS = 8


def lanes(shape):
    return lax.broadcasted_iota(I32, shape, len(shape) - 1)


def rows(shape):
    return lax.broadcasted_iota(I32, shape, len(shape) - 2)


def column(row, count, offset=0):
    shape = (count, row.shape[1])
    picked = jnp.where(lanes(shape) == rows(shape) + offset, jnp.broadcast_to(row, shape), 0.0)
    return jnp.sum(picked, axis=1, keepdims=True)


def silu(value):
    half = 0.5 * value
    return half + half * jnp.tanh(half)


def exact_dot(left, right):
    return jnp.dot(left, right, precision=HIGH, preferred_element_type=F32)


def dot(left, right):
    return jnp.dot(left, right, preferred_element_type=F32)


def split3(value):
    top = value.astype(BF16)
    rest = value - top.astype(F32)
    middle = rest.astype(BF16)
    return top, middle, (rest - middle.astype(F32)).astype(BF16)


def eliminate(step, system):
    sub = rows((PIVOTS, 128))

    def spread(block, k):
        return jnp.broadcast_to(block[k : k + 1], (PIVOTS, 128))

    columns = [jnp.broadcast_to(system[:, k : k + 1], system.shape) for k in range(PIVOTS)]
    corner = [column_k[0:PIVOTS] for column_k in columns]
    lines = system[0:PIVOTS]
    for k in range(PIVOTS):
        inverse = 1.0 / spread(corner[k], k)
        here = sub == k
        line = spread(lines, k) * inverse
        lines = jnp.where(here, line, lines - corner[k] * line)
        for j in range(k + 1, PIVOTS):
            entry = spread(corner[j], k) * inverse
            corner[j] = jnp.where(here, entry, corner[j] - corner[k] * entry)
    rest = system[PIVOTS:]
    for k in range(PIVOTS):
        rest = rest - columns[k][PIVOTS:] * lines[k : k + 1]
    return pltpu.roll(jnp.concatenate([rest, lines], axis=0), 128 - PIVOTS, 1)


def kernel(
    sizes,
    h_fld, h_oheads, h_ovar, h_noise, h_oindex, h_ocount, h_nbrs, h_gain, h_bias, h_conv1, h_bias1,
    h_conv2, h_bias2, h_rout,
    upd_out, head_out,
    oheads, ovar, noise, oindex, nbrs, gain, bias, conv1, bias1, conv2, bias2, rout,
    const, wcentre, square, tall, fx, joined, ht,
    halo_l, halo_r, field_all, halo_all, nbr_all, onehot_col, onehot_row, own_hot,
    obs_all, panel, tiles, recv_z, gram_rows, mix_rows, picks, recv_m,
    s_in, ready, s_halo, r_halo, s_fld, r_fld, s_fh, r_fh, s_nb, r_nb, s_a, r_a, s_pan, r_pan,
    s_ob, r_ob, s_z, r_z, s_gz, r_gz, s_gy, r_gy, s_mz, r_mz, s_my, r_my,
):
    ns, nm, nz = sizes
    nq = nm // 2
    members = nbrs.shape[0]
    slots = ovar.shape[1]
    ch = gain.shape[1]
    half = members
    s, m = lax.axis_index("space"), lax.axis_index("members")
    z, y = s // NY, lax.rem(s, NY)
    own = y * nz + z

    def copy(src, dst, send, recv, to_s, to_m):
        return pltpu.make_async_remote_copy(
            src_ref=src, dst_ref=dst, send_sem=send, recv_sem=recv,
            device_id={"space": to_s, "members": to_m}, device_id_type=pl.DeviceIdType.MESH,
        )

    def at_z(i):
        return lax.rem(z + i, nz)

    def at_y(i):
        return lax.rem(y + i, NY)

    def at_m(i):
        return lax.rem(m + i, nm)

    def each(count, action):
        def body(i, carry):
            action(i)
            return carry

        lax.fori_loop(1, count, body, 0)

    def each_far(action):
        def body(t, carry):
            action(nz // 2 + (t + 1) // 2 * (2 * lax.rem(t, 2) - 1))
            return carry

        lax.fori_loop(0, nz - 1, body, 0)

    loads = [
        pltpu.make_async_copy(src, dst, s_in.at[k])
        for k, (src, dst) in enumerate([
            (h_fld, field_all.at[m]), (h_gain, gain), (h_bias, bias), (h_bias1, bias1),
            (h_bias2, bias2), (h_rout, rout), (h_conv1, conv1), (h_conv2, conv2), (h_nbrs, nbrs),
            (h_ovar, ovar), (h_oheads, oheads), (h_noise, noise),
            (h_oindex, oindex),
        ])
    ]
    for load in loads:
        load.start()

    gate = pltpu.get_barrier_semaphore()

    def greet(to_s, to_m):
        pl.semaphore_signal(
            gate, inc=1, device_id={"space": to_s, "members": to_m},
            device_id_type=pl.DeviceIdType.MESH,
        )

    right, left = lax.rem(s + 1, ns), lax.rem(s + ns - 1, ns)
    for target in (right, left, at_z(1) * NY + y, at_z(nz - 1) * NY + y):
        greet(target, m)
    each(NY, lambda i: greet(z * NY + at_y(i), m))
    each(nm, lambda i: greet(s, at_m(i)))

    def tell(level, to_s):
        pl.semaphore_signal(
            ready.at[level], inc=1, device_id={"space": to_s, "members": m},
            device_id_type=pl.DeviceIdType.MESH,
        )

    def tell_z(level, distance):
        tell(level, at_z(distance) * NY + y)
        tell(level, at_z(nz - distance) * NY + y)

    for load in loads:
        load.wait()
    own_row = nbrs[pl.ds(own, 1), :]
    nbr_all[m] = jnp.zeros((8, 128), I32)
    nbr_all[m, :, 0:members] = jnp.broadcast_to(own_row, (8, members))
    pl.semaphore_wait(gate, 4 + (NY - 1) + (nm - 1))

    fld = field_all.at[m]
    to_right = copy(fld, halo_l, s_halo.at[0], r_halo.at[0], right, m)
    to_left = copy(fld, halo_r, s_halo.at[1], r_halo.at[1], left, m)
    to_right.start()
    to_left.start()
    each(NY, lambda i: tell(0, z * NY + at_y(i)))
    tell_z(1, 1)

    def nbr_copy(i):
        return copy(nbr_all.at[m], nbr_all.at[m], s_nb.at[i], r_nb.at[i], s, at_m(i))

    def field_copy(i):
        return copy(field_all.at[m], field_all.at[m], s_fld.at[i], r_fld.at[i], s, at_m(i))

    def halo_copy(i):
        return copy(halo_all.at[m], halo_all.at[m], s_fh.at[i], r_fh.at[i], s, at_m(i))

    each(nm, lambda i: nbr_copy(i).start())
    each(nm, lambda i: field_copy(i).start())

    wide = (ch, 128)
    const[0] = jnp.broadcast_to(column(gain[...], ch), wide)
    const[1] = jnp.broadcast_to(column(bias[...], ch), wide)
    const[2] = jnp.broadcast_to(column(bias1[...], ch), wide)
    const[3] = jnp.broadcast_to(column(bias2[...], ch), wide)
    read = rout[...].astype(F32).reshape(1, 3 * ch)
    const[4] = jnp.broadcast_to(column(read, ch, 2 * ch), wide)
    wcentre[0:ch, :] = conv2[1]
    wcentre[ch : ch + 16, :] = jnp.broadcast_to(read[:, 0 : 2 * ch], (16, 2 * ch)).astype(BF16)

    low = lanes((members, 128)) < half
    wide_lane = lanes((members, 128))
    low_row = lanes((1, 128)) < half
    keep_l = jnp.where(jnp.logical_and(low_row, s == 0), 0.0, 1.0)
    keep_r = jnp.where(jnp.logical_and(jnp.logical_not(low_row), s == ns - 1), 0.0, 1.0)

    def at(index):
        return pl.multiple_of(index * 128, 128)

    def lift_row(index):
        value = jnp.tanh(const[0] * fx[pl.ds(index + 5, 1), :] + const[1])
        joined[0:ch, pl.ds(at(index), 128)] = value.astype(BF16)

    def mask(top, index, keep):
        where = (slice(top, top + ch), slice(index * 128, index * 128 + 128))
        joined[where] = (joined[where].astype(F32) * keep).astype(BF16)

    def lift_inner(values):
        square[0:members, :] = values
        square[members : 2 * members, :] = values
        tall[8:136, :] = square[...].T
        fx[8:72, :] = jnp.where(lanes((64, 128)) < half, tall[8:72, :], tall[72:136, :])

        def block(k, carry):
            for inner in range(8):
                lift_row(3 + k * 8 + inner)
            return carry

        lax.fori_loop(0, 8, block, 0)

    def lift_outer(halos):
        square[0:members, :] = halos
        square[members : 2 * members, :] = halos
        turned = square[...].T
        near = lanes((8, 128)) < half
        fx[0:8, :] = jnp.where(near, turned[0:8, :], tall[64:72, :])
        fx[72:80, :] = jnp.where(near, tall[72:80, :], turned[8:16, :])
        for index in (0, 1, 2):
            lift_row(index)
            mask(0, index, keep_l)
        for index in (67, 68, 69):
            lift_row(index)
            mask(0, index, keep_r)

    def convolve():
        size = STEP * 128
        b1 = const[2][:, 0:1]
        b2 = const[3][:, 0:1]
        ro3 = const[4][:, 0:1]

        def middle(block, carry):
            base = block * STEP
            total = dot(conv1[0], joined[0:ch, pl.ds(at(base), size)])
            total += dot(conv1[1], joined[0:ch, pl.ds(at(base + 1), size)])
            total += dot(conv1[2], joined[0:ch, pl.ds(at(base + 2), size)])
            joined[ch : 2 * ch, pl.ds(at(base + 1), size)] = silu(total + b1).astype(BF16)
            return carry

        lax.fori_loop(0, 68 // STEP, middle, 0, unroll=68 // STEP)
        for index in (1, 2):
            mask(ch, index, keep_l)
        for index in (67, 68):
            mask(ch, index, keep_r)

        def last(block, carry):
            base = block * STEP
            centre = dot(wcentre[...], joined[:, pl.ds(at(base + 3), size)])
            total = centre[0:ch]
            total += dot(conv2[0], joined[:, pl.ds(at(base + 1), size)])
            total += dot(conv2[2], joined[:, pl.ds(at(base + 5), size)])
            third = silu(total + b2).astype(BF16).astype(F32)
            head = centre[ch : ch + 1] + jnp.sum(third * ro3, axis=0, keepdims=True)
            for inner in range(STEP):
                ht[pl.ds(base + inner, 1), :] = head[:, inner * 128 : inner * 128 + 128]
            return carry

        lax.fori_loop(0, 64 // STEP, last, 0, unroll=64 // STEP)

    lift_inner(fld[...])

    variance = ovar[...]
    live = lanes((1, slots)) < h_ocount[0]
    weight = jnp.where(live, 1.0 / variance, 0.0)
    tile_t = noise[...] * column(jnp.sqrt(variance), slots) + column(oheads[...], slots)
    obs_all[y, 0, :, 0:members] = tile_t
    obs_all[y, 0, :, members : 2 * members] = tile_t
    obs_all[y, 1] = jnp.broadcast_to(column(weight, slots), (slots, 128))

    def obs_copy(i):
        return copy(obs_all.at[y], obs_all.at[y], s_ob.at[i], r_ob.at[i], z * NY + at_y(i), m)

    each(NY, lambda i: obs_copy(i).start())
    pl.semaphore_wait(ready.at[1], 2)
    tell_z(2, 2)

    to_right.wait()
    to_left.wait()
    halo_all[m] = jnp.where(
        wide_lane < 8,
        pltpu.roll(halo_l[...], 8, 1),
        jnp.where(wide_lane < 16, pltpu.roll(halo_r[...], 8, 1), 0.0),
    )
    each(nm, lambda i: halo_copy(i).start())
    lift_outer(halo_all[m])
    convolve()

    cell = column(oindex[...].astype(F32), slots).astype(I32)
    narrow = (slots, 64)
    first_half = (lanes(narrow) == cell).astype(F32)
    second_half = (lanes(narrow) + 64 == cell).astype(F32)
    heads_t = ht[...]
    wide_obs = lanes((slots, 128))
    both = jnp.where(wide_obs < half, exact_dot(first_half, heads_t), exact_dot(second_half, heads_t))
    both = both + pltpu.roll(both, half, 1)
    upper = slots // 2
    panel[y, m] = jnp.where(lanes((upper, 128)) < half, both[0:upper], both[upper:slots])

    def panel_copy(i, j):
        here = panel.at[y, m]
        return copy(here, here, s_pan.at[i, j], r_pan.at[i, j], z * NY + at_y(i), at_m(j))

    def panel_block(i):
        here = panel.at[y]
        return copy(here, here, s_pan.at[i, 0], r_pan.at[i, 0], z * NY + at_y(i), m)

    def panel_part(i, j):
        here = panel.at[y, m]
        return copy(here, here, s_pan.at[i, 0], r_pan.at[i, 0], z * NY + at_y(i), at_m(j))

    pl.semaphore_wait(ready.at[0], NY - 1)

    def all_members(i):
        def body(j, carry):
            panel_part(i, j).start()
            return carry

        lax.fori_loop(0, nm, body, 0)

    each(NY, all_members)
    each(nm, lambda j: panel_copy(0, j).start())
    pl.semaphore_wait(ready.at[2], 2)
    tell_z(3, 4)

    own_ids = column(own_row.astype(F32), members).astype(I32)
    own_hot[...] = (lanes((members, nm * members)) == own_ids).astype(F32)
    each(nm, lambda j: panel_copy(0, j).wait_recv())
    each(NY, lambda i: panel_block(i).wait_recv())
    each(NY, lambda i: obs_copy(i).wait())

    depth = NY * slots
    deep = lanes((depth, 128)) < half
    packed_rows = NY * upper
    flat = [panel[:, g].reshape(packed_rows, 128) for g in range(nm)]
    swapped = [pltpu.roll(value, half, 1) for value in flat]
    front = lanes((packed_rows, 128)) < half

    def whole(first_part, second_part):
        first_part = first_part.reshape(NY, upper, 128)
        second_part = second_part.reshape(NY, upper, 128)
        return jnp.concatenate([first_part, second_part], axis=1).reshape(depth, 128)

    pairs = [
        whole(
            jnp.where(front, flat[2 * q], swapped[2 * q + 1]),
            jnp.where(front, swapped[2 * q], flat[2 * q + 1]),
        )
        for q in range(nq)
    ]
    total = pairs[0]
    for q in range(1, nq):
        total = total + pairs[q]
    centre = jnp.sum(total, axis=1, keepdims=True) / (nm * members)
    own_flat = panel[:, m].reshape(packed_rows, 128)
    own_swapped = pltpu.roll(own_flat, half, 1)
    mine = whole(
        jnp.where(front, own_flat, own_swapped), jnp.where(front, own_swapped, own_flat)
    )
    data = obs_all[:, 0].reshape(depth, 128)
    lead = obs_all[:, 1].reshape(depth, 128) * jnp.where(deep, mine - centre, data - mine)
    square[...] = lead.T
    first = pl.multiple_of(y * nz, nz)
    left_side = jnp.concatenate(
        [square[pl.ds(first, nz), :], square[pl.ds(members + first, nz), :]], axis=0
    )
    block = exact_dot(left_side, jnp.concatenate([pair - centre for pair in pairs], axis=1))
    for q in range(nq):
        tiles[:, q, :] = block[0:nz, q * 128 : q * 128 + 128]
        tiles[:, nq + q, :] = block[nz : 2 * nz, q * 128 : q * 128 + 128]

    def z_copy(i):
        return copy(tiles.at[at_z(i)], recv_z.at[i], s_z.at[i], r_z.at[i], at_z(i) * NY + y, m)

    pl.semaphore_wait(ready.at[3], 2)
    each_far(lambda i: z_copy(i).start())

    each(nm, lambda i: nbr_copy(i).wait())
    for pair in range(nq):
        lane_ids = jnp.where(
            low_row, nbr_all[2 * pair, 0:1, :], pltpu.roll(nbr_all[2 * pair + 1], half, 1)[0:1, :]
        )
        grid = (nm * members, 128)
        onehot_col[:, pair * 128 : pair * 128 + 128] = (rows(grid) == lane_ids).astype(F32).astype(BF16)
        ids = column(lane_ids.astype(F32), 128).astype(I32)
        fold = (128, 3 * members)
        onehot_row[pair * 128 : pair * 128 + 128, :] = (
            (jnp.bitwise_and(lanes(fold), members - 1) + m * members == ids).astype(F32).astype(BF16)
        )

    each(nz, lambda i: z_copy(i).wait_recv())
    own_tile = tiles[z]
    for i in range(1, nz):
        own_tile = own_tile + recv_z[i]

    def gather_rows(buffer, sz, rz, sy, ry, meanwhile):
        def by_z(i):
            here = buffer.at[y, z]
            return copy(here, here, sz.at[i], rz.at[i], at_z(i) * NY + y, m)

        def by_y(i, row):
            here = buffer.at[y, row]
            return copy(here, here, sy.at[i], ry.at[i], z * NY + at_y(i), m)

        def block(i):
            return copy(buffer.at[y], buffer.at[y], sy.at[i], ry.at[i], z * NY + at_y(i), m)

        each_far(lambda i: by_z(i).start())
        each(NY, lambda i: by_y(i, z).start())
        result = meanwhile()

        def onward(t, carry):
            near = t // 2 + 1
            i = near + lax.rem(t, 2) * (nz - 2 * near)
            by_z(i).wait_recv()
            row = lax.rem(z + nz - i, nz)
            for k in range(1, NY):
                by_y(k, row).start()
            return carry

        lax.fori_loop(0, nz - 1, onward, 0)
        each(NY, lambda i: block(i).wait_recv())

        def sent():
            each(nz, lambda i: by_z(i).wait_send())
            each(NY, lambda i: block(i).wait_send())

        return result, sent

    def right_side():
        value = jnp.zeros((members, 1), F32)
        for q in range(nq):
            line = jnp.broadcast_to(own_tile[nq + q : nq + q + 1], (members, 128))
            value = value + jnp.sum(line * own_hot[:, q * 128 : q * 128 + 128], axis=1, keepdims=True)
        return value - jnp.mean(value, axis=0, keepdims=True)

    gram_rows[y, z] = own_tile[0:nq]
    rhs, gram_sent = gather_rows(gram_rows, s_gz, r_gz, s_gy, r_gy, right_side)

    parts = [split3(gram_rows[:, :, q, :].reshape(members, 128)) for q in range(nq)]
    stacked = jnp.concatenate(
        [jnp.concatenate([parts[q][k] for q in range(nq)], axis=1) for k in range(3)], axis=0
    )
    chosen = dot(stacked, onehot_col[...])
    chosen = chosen[0:members] + (chosen[members : 2 * members] + chosen[2 * members : 3 * members])
    short = members // 2
    low_short = lanes((short, 128)) < half
    for pair in range(nq):
        lump = jnp.concatenate(split3(chosen[:, pair * 128 : pair * 128 + 128]), axis=0)
        picked = dot(onehot_row[pair * 128 : pair * 128 + 128, :], lump)
        turned = pltpu.roll(picked, half, 1)
        picks[2 * pair] = jnp.where(low_short, picked[0:short], turned[short:members])
        picks[2 * pair + 1] = jnp.where(
            low_short, turned[members : members + short], picked[members + short : 2 * members]
        )

    def pick_copy(i):
        return copy(picks.at[at_m(i)], recv_m.at[i], s_a.at[i], r_a.at[i], s, at_m(i))

    each(nm, lambda i: pick_copy(i).start())
    each(nm, lambda i: pick_copy(i).wait_recv())
    packed = picks[m]
    for i in range(1, nm):
        packed = packed + recv_m[i]
    gram = jnp.concatenate([packed, pltpu.roll(packed, half, 1)], axis=0)
    gram = jnp.where(low, gram, 0.0)
    row_mean = jnp.sum(gram, axis=1, keepdims=True) / members
    col_mean = jnp.sum(gram, axis=0, keepdims=True) / members
    all_mean = jnp.sum(row_mean, axis=0, keepdims=True) / members
    gram = jnp.where(low, gram - row_mean - col_mean + all_mean, 0.0)
    gram = gram + jnp.where(wide_lane == rows((members, 128)), members - 1.0, 0.0)
    gram = jnp.where(wide_lane == members, rhs, gram)

    solved = lax.fori_loop(0, members // PIVOTS, eliminate, gram)[:, 0:1]
    coef = solved - jnp.mean(solved, axis=0, keepdims=True)
    mix = jnp.sum(own_hot[...] * coef, axis=0, keepdims=True)
    for q in range(nq):
        mix_rows[y, z, q : q + 1] = mix[:, q * 128 : q * 128 + 128]

    def arrivals():
        each(nm, lambda i: field_copy(i).wait())
        each(nm, lambda i: halo_copy(i).wait())
        each(nm, lambda j: panel_copy(0, j).wait_send())
        each(NY, lambda i: panel_block(i).wait_send())
        each(nz, lambda i: z_copy(i).wait_send())
        each(nm, lambda i: pick_copy(i).wait_send())
        gram_sent()

    _, mix_sent = gather_rows(mix_rows, s_mz, r_mz, s_my, r_my, arrivals)

    updated = fld[...]
    halos = halo_all[m]
    for q in range(nq):
        part = mix_rows[:, :, q, :].reshape(members, 128)
        updated = updated + exact_dot(part, field_all[2 * q : 2 * q + 2].reshape(128, 128))
        halos = halos + exact_dot(part, halo_all[2 * q : 2 * q + 2].reshape(128, 128))
    upd_out[...] = updated
    mix_sent()
    lift_inner(updated)
    lift_outer(halos)
    convolve()
    square[0:members, :] = ht[...]
    square[members : 2 * members, :] = ht[...]
    turned = square[...].T
    head_out[...] = jnp.where(low, turned[0:members], turned[members : 2 * members])


def solution(mesh):
    ns, nm = mesh.shape["space"], mesh.shape["members"]
    nz, nq = ns // NY, nm // 2
    dma = pltpu.SemaphoreType.DMA
    vmem = pltpu.VMEM

    def on_device(
        log_field, obs_heads, obs_var, obs_noise, obs_index, obs_count, neighbours,
        lift_gain, lift_bias, conv_first, bias_first, conv_second, bias_second, readout,
    ):
        members, cells = log_field.shape
        slots = obs_var.shape[0]
        ch = lift_gain.shape[0]
        block = (members, 128)
        out = jax.ShapeDtypeStruct((members, cells), F32)
        in_vmem = pl.BlockSpec(memory_space=pltpu.VMEM)
        in_place = pl.BlockSpec(memory_space=pltpu.HBM)
        given = (
            log_field, obs_heads[None], obs_var[None], obs_noise.T, obs_index, obs_count,
            neighbours, lift_gain[None], lift_bias[None], conv_first, bias_first[None],
            conv_second, bias_second[None], readout,
        )
        scratch = [
            *[vmem(value.shape, value.dtype) for value in given[1:] if value.shape != (1,)],
            vmem((5, ch, 128), F32), vmem((ch + 16, 2 * ch), BF16), vmem((128, 128), F32),
            vmem((144, 128), F32), vmem((80, 128), F32), vmem((2 * ch, 70 * 128), BF16),
            vmem((64, 128), F32),
            vmem(block, F32), vmem(block, F32), vmem((nm, *block), F32), vmem((nm, *block), F32),
            vmem((nm, 8, 128), I32), vmem((nm * members, nm * members), BF16),
            vmem((nm * members, 3 * members), BF16), vmem((members, nm * members), F32),
            vmem((NY, 2, slots, 128), F32), vmem((NY, nm, slots // 2, 128), F32),
            vmem((nz, nm, 128), F32), vmem((nz, nm, 128), F32),
            vmem((NY, nz, nq, 128), F32), vmem((NY, nz, nq, 128), F32),
            vmem((nm, members // 2, 128), F32), vmem((nm, members // 2, 128), F32),
            dma((len(given) - 1,)), pltpu.SemaphoreType.REGULAR((4,)), dma((2,)), dma((2,)),
            *[dma((nm,))] * 8,
            dma((NY, nm)), dma((NY, nm)),
            dma((NY,)), dma((NY,)), dma((nz,)), dma((nz,)),
            dma((nz,)), dma((nz,)), dma((NY,)), dma((NY,)),
            dma((nz,)), dma((nz,)), dma((NY,)), dma((NY,)),
        ]

        def body(*refs):
            kernel((ns, nm, nz), *refs)

        return pl.pallas_call(
            body,
            out_shape=(out, out),
            in_specs=[
                pl.BlockSpec(memory_space=pltpu.SMEM) if value.shape == (1,) else in_place
                for value in given
            ],
            out_specs=(in_vmem, in_vmem),
            scratch_shapes=scratch,
            name="smoother",
            compiler_params=pltpu.CompilerParams(
                collective_id=0, has_side_effects=True, vmem_limit_bytes=32 * 1024 * 1024
            ),
        )(*[
            value if value.shape == (1,) else pltpu.with_memory_space_constraint(value, pltpu.HBM)
            for value in given
        ])

    in_specs = (
        P("members", "space"), P("space"), P("space"), P("members", "space"), P("space", None),
        P("space"), P("members", None), P(), P(), P(), P(), P(), P(), P(),
    )
    out_specs = (P("members", "space"), P("members", "space"))
    return jax.shard_map(
        on_device, mesh=mesh, in_specs=in_specs, out_specs=out_specs, check_vma=False
    )
```

```python
import jax
import jax.numpy as jnp
from jax import lax
from jax.experimental import pallas as pl
from jax.experimental.pallas import tpu as pltpu
from jax.sharding import PartitionSpec as P

F32, BF16, I32 = jnp.float32, jnp.bfloat16, jnp.int32
HIGH = lax.Precision.HIGHEST
NY = 4
STEP = 4
PIVOTS = 8


def lanes(shape):
    return lax.broadcasted_iota(I32, shape, len(shape) - 1)


def rows(shape):
    return lax.broadcasted_iota(I32, shape, len(shape) - 2)


def column(row, count, offset=0):
    shape = (count, row.shape[1])
    picked = jnp.where(lanes(shape) == rows(shape) + offset, jnp.broadcast_to(row, shape), 0.0)
    return jnp.sum(picked, axis=1, keepdims=True)


def silu(value):
    half = 0.5 * value
    return half + half * jnp.tanh(half)


def exact_dot(left, right):
    return jnp.dot(left, right, precision=HIGH, preferred_element_type=F32)


def dot(left, right):
    return jnp.dot(left, right, preferred_element_type=F32)


def split3(value):
    top = value.astype(BF16)
    rest = value - top.astype(F32)
    middle = rest.astype(BF16)
    return top, middle, (rest - middle.astype(F32)).astype(BF16)


def eliminate(step, system):
    sub = rows((PIVOTS, 128))

    def spread(block, k):
        return jnp.broadcast_to(block[k : k + 1], (PIVOTS, 128))

    columns = [jnp.broadcast_to(system[:, k : k + 1], system.shape) for k in range(PIVOTS)]
    corner = [column_k[0:PIVOTS] for column_k in columns]
    lines = system[0:PIVOTS]
    for k in range(PIVOTS):
        inverse = 1.0 / spread(corner[k], k)
        here = sub == k
        line = spread(lines, k) * inverse
        lines = jnp.where(here, line, lines - corner[k] * line)
        for j in range(k + 1, PIVOTS):
            entry = spread(corner[j], k) * inverse
            corner[j] = jnp.where(here, entry, corner[j] - corner[k] * entry)
    rest = system[PIVOTS:]
    for k in range(PIVOTS):
        rest = rest - columns[k][PIVOTS:] * lines[k : k + 1]
    return pltpu.roll(jnp.concatenate([rest, lines], axis=0), 128 - PIVOTS, 1)


def kernel(
    sizes,
    h_fld, h_oheads, h_ovar, h_noise, h_oindex, h_ocount, h_nbrs, h_gain, h_bias, h_conv1, h_bias1,
    h_conv2, h_bias2, h_rout,
    upd_out, head_out,
    oheads, ovar, noise, oindex, nbrs, gain, bias, conv1, bias1, conv2, bias2, rout,
    const, wcentre, square, tall, fx, joined, ht,
    halo_l, halo_r, field_all, halo_all, nbr_all, onehot_col, onehot_row, own_hot,
    obs_all, panel, tiles, recv_z, sides, recv_s, gram_rows, mix_rows, picks, recv_m,
    s_in, ready, s_halo, r_halo, s_fld, r_fld, s_fh, r_fh, s_nb, r_nb, s_a, r_a, s_pan, r_pan,
    s_ob, r_ob, s_z, r_z, s_s, r_s, s_gz, r_gz, s_gy, r_gy, s_mz, r_mz, s_my, r_my,
):
    ns, nm, nz = sizes
    nq = nm // 2
    members = nbrs.shape[0]
    slots = ovar.shape[1]
    ch = gain.shape[1]
    half = members
    s, m = lax.axis_index("space"), lax.axis_index("members")
    z, y = s // NY, lax.rem(s, NY)
    own = y * nz + z

    def copy(src, dst, send, recv, to_s, to_m):
        return pltpu.make_async_remote_copy(
            src_ref=src, dst_ref=dst, send_sem=send, recv_sem=recv,
            device_id={"space": to_s, "members": to_m}, device_id_type=pl.DeviceIdType.MESH,
        )

    def at_z(i):
        return lax.rem(z + i, nz)

    def at_y(i):
        return lax.rem(y + i, NY)

    def at_m(i):
        return lax.rem(m + i, nm)

    def each(count, action):
        def body(i, carry):
            action(i)
            return carry

        lax.fori_loop(1, count, body, 0)

    def each_far(action):
        def body(t, carry):
            action(nz // 2 + (t + 1) // 2 * (2 * lax.rem(t, 2) - 1))
            return carry

        lax.fori_loop(0, nz - 1, body, 0)

    gate = pltpu.get_barrier_semaphore()

    def greet(to_s, to_m):
        pl.semaphore_signal(
            gate, inc=1, device_id={"space": to_s, "members": to_m},
            device_id_type=pl.DeviceIdType.MESH,
        )

    right, left = lax.rem(s + 1, ns), lax.rem(s + ns - 1, ns)
    for target in (right, left, at_z(1) * NY + y, at_z(nz - 1) * NY + y):
        greet(target, m)
    each(NY, lambda i: greet(z * NY + at_y(i), m))
    each(nm, lambda i: greet(s, at_m(i)))

    loads = [
        pltpu.make_async_copy(src, dst, s_in.at[k])
        for k, (src, dst) in enumerate([
            (h_fld, field_all.at[m]), (h_gain, gain), (h_bias, bias), (h_bias1, bias1),
            (h_bias2, bias2), (h_rout, rout), (h_conv1, conv1), (h_conv2, conv2), (h_nbrs, nbrs),
            (h_ovar, ovar), (h_oheads, oheads), (h_noise, noise),
            (h_oindex, oindex),
        ])
    ]
    for load in loads:
        load.start()

    def tell(level, to_s):
        pl.semaphore_signal(
            ready.at[level], inc=1, device_id={"space": to_s, "members": m},
            device_id_type=pl.DeviceIdType.MESH,
        )

    def tell_z(level, distance):
        tell(level, at_z(distance) * NY + y)
        tell(level, at_z(nz - distance) * NY + y)

    loads[0].wait()
    pl.semaphore_wait(gate, 4 + (NY - 1) + (nm - 1))

    fld = field_all.at[m]
    to_right = copy(fld, halo_l, s_halo.at[0], r_halo.at[0], right, m)
    to_left = copy(fld, halo_r, s_halo.at[1], r_halo.at[1], left, m)
    to_right.start()
    to_left.start()
    each(NY, lambda i: tell(0, z * NY + at_y(i)))
    tell_z(1, 1)

    def nbr_copy(i):
        return copy(nbr_all.at[m], nbr_all.at[m], s_nb.at[i], r_nb.at[i], s, at_m(i))

    def field_copy(i):
        return copy(field_all.at[m], field_all.at[m], s_fld.at[i], r_fld.at[i], s, at_m(i))

    def halo_copy(i):
        return copy(halo_all.at[m], halo_all.at[m], s_fh.at[i], r_fh.at[i], s, at_m(i))

    for load in loads[1:]:
        load.wait()
    own_row = nbrs[pl.ds(own, 1), :]
    nbr_all[m] = jnp.zeros((8, 128), I32)
    nbr_all[m, :, 0:members] = jnp.broadcast_to(own_row, (8, members))
    each(nm, lambda i: nbr_copy(i).start())

    wide = (ch, 128)
    const[0] = jnp.broadcast_to(column(gain[...], ch), wide)
    const[1] = jnp.broadcast_to(column(bias[...], ch), wide)
    const[2] = jnp.broadcast_to(column(bias1[...], ch), wide)
    const[3] = jnp.broadcast_to(column(bias2[...], ch), wide)
    read = rout[...].astype(F32).reshape(1, 3 * ch)
    const[4] = jnp.broadcast_to(column(read, ch, 2 * ch), wide)
    wcentre[0:ch, :] = conv2[1]
    wcentre[ch : ch + 16, :] = jnp.broadcast_to(read[:, 0 : 2 * ch], (16, 2 * ch)).astype(BF16)

    low = lanes((members, 128)) < half
    wide_lane = lanes((members, 128))
    low_row = lanes((1, 128)) < half
    keep_l = jnp.where(jnp.logical_and(low_row, s == 0), 0.0, 1.0)
    keep_r = jnp.where(jnp.logical_and(jnp.logical_not(low_row), s == ns - 1), 0.0, 1.0)

    def at(index):
        return pl.multiple_of(index * 128, 128)

    def lift_row(index):
        value = jnp.tanh(const[0] * fx[pl.ds(index + 5, 1), :] + const[1])
        joined[0:ch, pl.ds(at(index), 128)] = value.astype(BF16)

    def mask(top, index, keep):
        where = (slice(top, top + ch), slice(index * 128, index * 128 + 128))
        joined[where] = (joined[where].astype(F32) * keep).astype(BF16)

    def lift_inner(values):
        square[0:members, :] = values
        square[members : 2 * members, :] = values
        tall[8:136, :] = square[...].T
        fx[8:72, :] = jnp.where(lanes((64, 128)) < half, tall[8:72, :], tall[72:136, :])

        def block(k, carry):
            for inner in range(8):
                lift_row(3 + k * 8 + inner)
            return carry

        lax.fori_loop(0, 8, block, 0)

    def lift_outer(halos):
        square[0:members, :] = halos
        square[members : 2 * members, :] = halos
        turned = square[...].T
        near = lanes((8, 128)) < half
        fx[0:8, :] = jnp.where(near, turned[0:8, :], tall[64:72, :])
        fx[72:80, :] = jnp.where(near, tall[72:80, :], turned[8:16, :])
        for index in (0, 1, 2):
            lift_row(index)
            mask(0, index, keep_l)
        for index in (67, 68, 69):
            lift_row(index)
            mask(0, index, keep_r)

    size = STEP * 128

    def middle(block, carry=0):
        base = block * STEP
        total = dot(conv1[0], joined[0:ch, pl.ds(at(base), size)])
        total += dot(conv1[1], joined[0:ch, pl.ds(at(base + 1), size)])
        total += dot(conv1[2], joined[0:ch, pl.ds(at(base + 2), size)])
        joined[ch : 2 * ch, pl.ds(at(base + 1), size)] = silu(total + const[2][:, 0:1]).astype(BF16)
        return carry

    def last(block, carry=0):
        base = block * STEP
        centre = dot(wcentre[...], joined[:, pl.ds(at(base + 3), size)])
        total = centre[0:ch]
        total += dot(conv2[0], joined[:, pl.ds(at(base + 1), size)])
        total += dot(conv2[2], joined[:, pl.ds(at(base + 5), size)])
        third = silu(total + const[3][:, 0:1]).astype(BF16).astype(F32)
        head = centre[ch : ch + 1] + jnp.sum(third * const[4][:, 0:1], axis=0, keepdims=True)
        for inner in range(STEP):
            ht[pl.ds(base + inner, 1), :] = head[:, inner * 128 : inner * 128 + 128]
        return carry

    mids, ends = 68 // STEP, 64 // STEP

    def conv_inner():
        lax.fori_loop(1, mids - 1, middle, 0, unroll=mids - 2)
        lax.fori_loop(1, ends - 1, last, 0, unroll=ends - 2)

    def conv_outer():
        middle(0)
        middle(mids - 1)
        for index in (1, 2):
            mask(ch, index, keep_l)
        for index in (67, 68):
            mask(ch, index, keep_r)
        last(0)
        last(ends - 1)

    lift_inner(fld[...])
    conv_inner()

    pl.semaphore_wait(ready.at[1], 2)
    tell_z(2, 2)

    to_right.wait()
    to_left.wait()
    halo_all[m] = jnp.where(
        wide_lane < 8,
        pltpu.roll(halo_l[...], 8, 1),
        jnp.where(wide_lane < 16, pltpu.roll(halo_r[...], 8, 1), 0.0),
    )
    lift_outer(halo_all[m])
    conv_outer()

    cell = column(oindex[...].astype(F32), slots).astype(I32)
    narrow = (slots, 64)
    first_half = (lanes(narrow) == cell).astype(F32)
    second_half = (lanes(narrow) + 64 == cell).astype(F32)
    heads_t = ht[...]
    wide_obs = lanes((slots, 128))
    both = jnp.where(wide_obs < half, exact_dot(first_half, heads_t), exact_dot(second_half, heads_t))
    both = both + pltpu.roll(both, half, 1)
    upper = slots // 2
    panel[y, m] = jnp.where(lanes((upper, 128)) < half, both[0:upper], both[upper:slots])

    def panel_copy(i, j):
        here = panel.at[y, m]
        return copy(here, here, s_pan.at[i, j], r_pan.at[i, j], z * NY + at_y(i), at_m(j))

    def panel_block(i):
        here = panel.at[y]
        return copy(here, here, s_pan.at[i, 0], r_pan.at[i, 0], z * NY + at_y(i), m)

    def panel_part(i, j):
        here = panel.at[y, m]
        return copy(here, here, s_pan.at[i, 0], r_pan.at[i, 0], z * NY + at_y(i), at_m(j))

    pl.semaphore_wait(ready.at[0], NY - 1)

    def all_members(i):
        def body(j, carry):
            panel_part(i, j).start()
            return carry

        lax.fori_loop(0, nm, body, 0)

    each(NY, all_members)
    each(nm, lambda j: panel_copy(0, j).start())
    variance = ovar[...]
    live = lanes((1, slots)) < h_ocount[0]
    weight = jnp.where(live, 1.0 / variance, 0.0)
    tile_t = noise[...] * column(jnp.sqrt(variance), slots) + column(oheads[...], slots)
    obs_all[y, 0, :, 0:members] = tile_t
    obs_all[y, 0, :, members : 2 * members] = tile_t
    obs_all[y, 1] = jnp.broadcast_to(column(weight, slots), (slots, 128))

    def obs_copy(i):
        return copy(obs_all.at[y], obs_all.at[y], s_ob.at[i], r_ob.at[i], z * NY + at_y(i), m)

    each(NY, lambda i: obs_copy(i).start())
    pl.semaphore_wait(ready.at[2], 2)
    tell_z(3, 4)

    each(nm, lambda j: panel_copy(0, j).wait_recv())
    each(NY, lambda i: panel_block(i).wait_recv())
    each(NY, lambda i: obs_copy(i).wait())

    depth = NY * slots
    deep = lanes((depth, 128)) < half
    packed_rows = NY * upper
    flat = [panel[:, g].reshape(packed_rows, 128) for g in range(nm)]
    swapped = [pltpu.roll(value, half, 1) for value in flat]
    front = lanes((packed_rows, 128)) < half

    def whole(first_part, second_part):
        first_part = first_part.reshape(NY, upper, 128)
        second_part = second_part.reshape(NY, upper, 128)
        return jnp.concatenate([first_part, second_part], axis=1).reshape(depth, 128)

    pairs = [
        whole(
            jnp.where(front, flat[2 * q], swapped[2 * q + 1]),
            jnp.where(front, swapped[2 * q], flat[2 * q + 1]),
        )
        for q in range(nq)
    ]
    total = pairs[0]
    for q in range(1, nq):
        total = total + pairs[q]
    centre = jnp.sum(total, axis=1, keepdims=True) / (nm * members)
    own_flat = panel[:, m].reshape(packed_rows, 128)
    own_swapped = pltpu.roll(own_flat, half, 1)
    mine = whole(
        jnp.where(front, own_flat, own_swapped), jnp.where(front, own_swapped, own_flat)
    )
    data = obs_all[:, 0].reshape(depth, 128)
    lead = obs_all[:, 1].reshape(depth, 128) * jnp.where(deep, mine - centre, data - mine)
    square[...] = lead.T
    first = pl.multiple_of(y * nz, nz)
    left_side = jnp.concatenate(
        [square[pl.ds(first, nz), :], square[pl.ds(members + first, nz), :]], axis=0
    )
    block = exact_dot(left_side, jnp.concatenate([pair - centre for pair in pairs], axis=1))
    for q in range(nq):
        tiles[:, q, :] = block[0:nz, q * 128 : q * 128 + 128]
        sides[:, q, :] = block[nz : 2 * nz, q * 128 : q * 128 + 128]

    def z_copy(i):
        return copy(tiles.at[at_z(i)], recv_z.at[i], s_z.at[i], r_z.at[i], at_z(i) * NY + y, m)

    def side_copy(i):
        return copy(sides.at[at_z(i)], recv_s.at[i], s_s.at[i], r_s.at[i], at_z(i) * NY + y, m)

    pl.semaphore_wait(ready.at[3], 2)
    each_far(lambda i: z_copy(i).start())
    each_far(lambda i: side_copy(i).start())
    each(nm, lambda i: field_copy(i).start())
    each(nm, lambda i: halo_copy(i).start())

    own_ids = column(own_row.astype(F32), members).astype(I32)
    own_hot[...] = (lanes((members, nm * members)) == own_ids).astype(F32)
    each(nm, lambda i: nbr_copy(i).wait())
    for pair in range(nq):
        lane_ids = jnp.where(
            low_row, nbr_all[2 * pair, 0:1, :], pltpu.roll(nbr_all[2 * pair + 1], half, 1)[0:1, :]
        )
        grid = (nm * members, 128)
        onehot_col[:, pair * 128 : pair * 128 + 128] = (rows(grid) == lane_ids).astype(F32).astype(BF16)
        ids = column(lane_ids.astype(F32), 128).astype(I32)
        fold = (128, 3 * members)
        onehot_row[pair * 128 : pair * 128 + 128, :] = (
            (jnp.bitwise_and(lanes(fold), members - 1) + m * members == ids).astype(F32).astype(BF16)
        )

    each(nz, lambda i: z_copy(i).wait_recv())
    own_tile = tiles[z]
    for i in range(1, nz):
        own_tile = own_tile + recv_z[i]

    def gather_rows(buffer, sz, rz, sy, ry, meanwhile):
        def by_z(i):
            here = buffer.at[y, z]
            return copy(here, here, sz.at[i], rz.at[i], at_z(i) * NY + y, m)

        def by_y(i, row):
            here = buffer.at[y, row]
            return copy(here, here, sy.at[i], ry.at[i], z * NY + at_y(i), m)

        def block(i):
            return copy(buffer.at[y], buffer.at[y], sy.at[i], ry.at[i], z * NY + at_y(i), m)

        each_far(lambda i: by_z(i).start())
        each(NY, lambda i: by_y(i, z).start())
        result = meanwhile()

        def onward(t, carry):
            near = t // 2 + 1
            i = near + lax.rem(t, 2) * (nz - 2 * near)
            by_z(i).wait_recv()
            row = lax.rem(z + nz - i, nz)
            for k in range(1, NY):
                by_y(k, row).start()
            return carry

        lax.fori_loop(0, nz - 1, onward, 0)
        each(NY, lambda i: block(i).wait_recv())

        def sent():
            each(nz, lambda i: by_z(i).wait_send())
            each(NY, lambda i: block(i).wait_send())

        return result, sent

    def right_side():
        each(nz, lambda i: side_copy(i).wait_recv())
        side = sides[z]
        for i in range(1, nz):
            side = side + recv_s[i]
        value = jnp.zeros((members, 1), F32)
        for q in range(nq):
            line = jnp.broadcast_to(side[q : q + 1], (members, 128))
            value = value + jnp.sum(line * own_hot[:, q * 128 : q * 128 + 128], axis=1, keepdims=True)
        return value - jnp.mean(value, axis=0, keepdims=True)

    gram_rows[y, z] = own_tile
    rhs, gram_sent = gather_rows(gram_rows, s_gz, r_gz, s_gy, r_gy, right_side)

    parts = [split3(gram_rows[:, :, q, :].reshape(members, 128)) for q in range(nq)]
    stacked = jnp.concatenate(
        [jnp.concatenate([parts[q][k] for q in range(nq)], axis=1) for k in range(3)], axis=0
    )
    chosen = dot(stacked, onehot_col[...])
    chosen = chosen[0:members] + (chosen[members : 2 * members] + chosen[2 * members : 3 * members])
    short = members // 2
    low_short = lanes((short, 128)) < half
    for pair in range(nq):
        lump = jnp.concatenate(split3(chosen[:, pair * 128 : pair * 128 + 128]), axis=0)
        picked = dot(onehot_row[pair * 128 : pair * 128 + 128, :], lump)
        turned = pltpu.roll(picked, half, 1)
        picks[2 * pair] = jnp.where(low_short, picked[0:short], turned[short:members])
        picks[2 * pair + 1] = jnp.where(
            low_short, turned[members : members + short], picked[members + short : 2 * members]
        )

    def pick_copy(i):
        return copy(picks.at[at_m(i)], recv_m.at[i], s_a.at[i], r_a.at[i], s, at_m(i))

    each(nm, lambda i: pick_copy(i).start())
    each(nm, lambda i: pick_copy(i).wait_recv())
    packed = picks[m]
    for i in range(1, nm):
        packed = packed + recv_m[i]
    gram = jnp.concatenate([packed, pltpu.roll(packed, half, 1)], axis=0)
    gram = jnp.where(low, gram, 0.0)
    row_mean = jnp.sum(gram, axis=1, keepdims=True) / members
    col_mean = jnp.sum(gram, axis=0, keepdims=True) / members
    all_mean = jnp.sum(row_mean, axis=0, keepdims=True) / members
    gram = jnp.where(low, gram - row_mean - col_mean + all_mean, 0.0)
    gram = gram + jnp.where(wide_lane == rows((members, 128)), members - 1.0, 0.0)
    gram = jnp.where(wide_lane == members, rhs, gram)

    solved = lax.fori_loop(0, members // PIVOTS, eliminate, gram)[:, 0:1]
    coef = solved - jnp.mean(solved, axis=0, keepdims=True)
    mix = jnp.sum(own_hot[...] * coef, axis=0, keepdims=True)
    for q in range(nq):
        mix_rows[y, z, q : q + 1] = mix[:, q * 128 : q * 128 + 128]

    def arrivals():
        each(nm, lambda i: field_copy(i).wait())
        each(nm, lambda i: halo_copy(i).wait())
        each(nm, lambda j: panel_copy(0, j).wait_send())
        each(NY, lambda i: panel_block(i).wait_send())
        each(nz, lambda i: z_copy(i).wait_send())
        each(nz, lambda i: side_copy(i).wait_send())
        each(nm, lambda i: pick_copy(i).wait_send())
        gram_sent()

    _, mix_sent = gather_rows(mix_rows, s_mz, r_mz, s_my, r_my, arrivals)

    updated = fld[...]
    halos = halo_all[m]
    for q in range(nq):
        part = mix_rows[:, :, q, :].reshape(members, 128)
        updated = updated + exact_dot(part, field_all[2 * q : 2 * q + 2].reshape(128, 128))
        halos = halos + exact_dot(part, halo_all[2 * q : 2 * q + 2].reshape(128, 128))
    upd_out[...] = updated
    mix_sent()
    lift_inner(updated)
    lift_outer(halos)
    conv_inner()
    conv_outer()
    square[0:members, :] = ht[...]
    square[members : 2 * members, :] = ht[...]
    turned = square[...].T
    head_out[...] = jnp.where(low, turned[0:members], turned[members : 2 * members])


def solution(mesh):
    ns, nm = mesh.shape["space"], mesh.shape["members"]
    nz, nq = ns // NY, nm // 2
    dma = pltpu.SemaphoreType.DMA
    vmem = pltpu.VMEM

    def on_device(
        log_field, obs_heads, obs_var, obs_noise, obs_index, obs_count, neighbours,
        lift_gain, lift_bias, conv_first, bias_first, conv_second, bias_second, readout,
    ):
        members, cells = log_field.shape
        slots = obs_var.shape[0]
        ch = lift_gain.shape[0]
        block = (members, 128)
        out = jax.ShapeDtypeStruct((members, cells), F32)
        in_vmem = pl.BlockSpec(memory_space=pltpu.VMEM)
        in_place = pl.BlockSpec(memory_space=pltpu.HBM)
        given = (
            log_field, obs_heads[None], obs_var[None], obs_noise.T, obs_index, obs_count,
            neighbours, lift_gain[None], lift_bias[None], conv_first, bias_first[None],
            conv_second, bias_second[None], readout,
        )
        scratch = [
            *[vmem(value.shape, value.dtype) for value in given[1:] if value.shape != (1,)],
            vmem((5, ch, 128), F32), vmem((ch + 16, 2 * ch), BF16), vmem((128, 128), F32),
            vmem((144, 128), F32), vmem((80, 128), F32), vmem((2 * ch, 70 * 128), BF16),
            vmem((64, 128), F32),
            vmem(block, F32), vmem(block, F32), vmem((nm, *block), F32), vmem((nm, *block), F32),
            vmem((nm, 8, 128), I32), vmem((nm * members, nm * members), BF16),
            vmem((nm * members, 3 * members), BF16), vmem((members, nm * members), F32),
            vmem((NY, 2, slots, 128), F32), vmem((NY, nm, slots // 2, 128), F32),
            *[vmem((nz, nq, 128), F32)] * 4,
            vmem((NY, nz, nq, 128), F32), vmem((NY, nz, nq, 128), F32),
            vmem((nm, members // 2, 128), F32), vmem((nm, members // 2, 128), F32),
            dma((len(given) - 1,)), pltpu.SemaphoreType.REGULAR((4,)), dma((2,)), dma((2,)),
            *[dma((nm,))] * 8,
            dma((NY, nm)), dma((NY, nm)),
            dma((NY,)), dma((NY,)), *[dma((nz,))] * 4,
            dma((nz,)), dma((nz,)), dma((NY,)), dma((NY,)),
            dma((nz,)), dma((nz,)), dma((NY,)), dma((NY,)),
        ]

        def body(*refs):
            kernel((ns, nm, nz), *refs)

        return pl.pallas_call(
            body,
            out_shape=(out, out),
            in_specs=[
                pl.BlockSpec(memory_space=pltpu.SMEM) if value.shape == (1,) else in_place
                for value in given
            ],
            out_specs=(in_vmem, in_vmem),
            scratch_shapes=scratch,
            name="smoother",
            compiler_params=pltpu.CompilerParams(
                collective_id=0, has_side_effects=True, vmem_limit_bytes=32 * 1024 * 1024
            ),
        )(*[
            value if value.shape == (1,) else pltpu.with_memory_space_constraint(value, pltpu.HBM)
            for value in given
        ])

    in_specs = (
        P("members", "space"), P("space"), P("space"), P("members", "space"), P("space", None),
        P("space"), P("members", None), P(), P(), P(), P(), P(), P(), P(),
    )
    out_specs = (P("members", "space"), P("members", "space"))
    return jax.shard_map(
        on_device, mesh=mesh, in_specs=in_specs, out_specs=out_specs, check_vma=False
    )
```

```python
import jax
import jax.numpy as jnp
from jax import lax
from jax.experimental import pallas as pl
from jax.experimental.pallas import tpu as pltpu
from jax.sharding import PartitionSpec as P

F32, BF16, I32 = jnp.float32, jnp.bfloat16, jnp.int32
HIGH = lax.Precision.HIGHEST
NY = 4
STEP = 4
PIVOTS = 8


def lanes(shape):
    return lax.broadcasted_iota(I32, shape, len(shape) - 1)


def rows(shape):
    return lax.broadcasted_iota(I32, shape, len(shape) - 2)


def column(row, count, offset=0):
    shape = (count, row.shape[1])
    picked = jnp.where(lanes(shape) == rows(shape) + offset, jnp.broadcast_to(row, shape), 0.0)
    return jnp.sum(picked, axis=1, keepdims=True)


def silu(value):
    half = 0.5 * value
    return half + half * jnp.tanh(half)


def exact_dot(left, right):
    return jnp.dot(left, right, precision=HIGH, preferred_element_type=F32)


def dot(left, right):
    return jnp.dot(left, right, preferred_element_type=F32)


def split3(value):
    top = value.astype(BF16)
    rest = value - top.astype(F32)
    middle = rest.astype(BF16)
    return top, middle, (rest - middle.astype(F32)).astype(BF16)


def eliminate(step, system):
    sub = rows((PIVOTS, 128))

    def spread(block, k):
        return jnp.broadcast_to(block[k : k + 1], (PIVOTS, 128))

    columns = [jnp.broadcast_to(system[:, k : k + 1], system.shape) for k in range(PIVOTS)]
    corner = [column_k[0:PIVOTS] for column_k in columns]
    lines = system[0:PIVOTS]
    for k in range(PIVOTS):
        inverse = 1.0 / spread(corner[k], k)
        here = sub == k
        line = spread(lines, k) * inverse
        lines = jnp.where(here, line, lines - corner[k] * line)
        for j in range(k + 1, PIVOTS):
            entry = spread(corner[j], k) * inverse
            corner[j] = jnp.where(here, entry, corner[j] - corner[k] * entry)
    rest = system[PIVOTS:]
    for k in range(PIVOTS):
        rest = rest - columns[k][PIVOTS:] * lines[k : k + 1]
    return pltpu.roll(jnp.concatenate([rest, lines], axis=0), 128 - PIVOTS, 1)


def kernel(
    sizes,
    h_fld, h_oheads, h_ovar, h_noise, h_oindex, h_ocount, h_nbrs, h_gain, h_bias, h_conv1, h_bias1,
    h_conv2, h_bias2, h_rout,
    upd_out, head_out,
    oheads, ovar, noise, oindex, nbrs, gain, bias, conv1, bias1, conv2, bias2, rout,
    const, wcentre, square, tall, fx, joined, ht,
    field_all, halo_all, nbr_all, onehot_col, onehot_row, own_hot,
    obs_all, panel, tiles, recv_z, sides, recv_s, gram_rows, mix_rows, picks, recv_m,
    s_in, ready, s_halo, r_halo, s_fld, r_fld, s_fh, r_fh, s_nb, r_nb, s_a, r_a, s_pan, r_pan,
    s_ob, r_ob, s_z, r_z, s_s, r_s, s_gz, r_gz, s_gy, r_gy, s_mz, r_mz, s_my, r_my,
):
    ns, nm, nz = sizes
    nq = nm // 2
    members = nbrs.shape[0]
    slots = ovar.shape[1]
    ch = gain.shape[1]
    half = members
    s, m = lax.axis_index("space"), lax.axis_index("members")
    z, y = s // NY, lax.rem(s, NY)
    own = y * nz + z

    def copy(src, dst, send, recv, to_s, to_m):
        return pltpu.make_async_remote_copy(
            src_ref=src, dst_ref=dst, send_sem=send, recv_sem=recv,
            device_id={"space": to_s, "members": to_m}, device_id_type=pl.DeviceIdType.MESH,
        )

    def at_z(i):
        return lax.rem(z + i, nz)

    def at_y(i):
        return lax.rem(y + i, NY)

    def at_m(i):
        return lax.rem(m + i, nm)

    def each(count, action):
        def body(i, carry):
            action(i)
            return carry

        lax.fori_loop(1, count, body, 0)

    def each_far(action):
        def body(t, carry):
            action(nz // 2 + (t + 1) // 2 * (2 * lax.rem(t, 2) - 1))
            return carry

        lax.fori_loop(0, nz - 1, body, 0)

    gate = pltpu.get_barrier_semaphore()

    def greet(to_s, to_m):
        pl.semaphore_signal(
            gate, inc=1, device_id={"space": to_s, "members": to_m},
            device_id_type=pl.DeviceIdType.MESH,
        )

    right, left = lax.rem(s + 1, ns), lax.rem(s + ns - 1, ns)
    for target in (right, left, at_z(1) * NY + y, at_z(nz - 1) * NY + y):
        greet(target, m)
    each(NY, lambda i: greet(z * NY + at_y(i), m))
    each(nm, lambda i: greet(s, at_m(i)))

    loads = [
        pltpu.make_async_copy(src, dst, s_in.at[k])
        for k, (src, dst) in enumerate([
            (h_fld, field_all.at[m]), (h_gain, gain), (h_bias, bias), (h_bias1, bias1),
            (h_bias2, bias2), (h_rout, rout), (h_conv1, conv1), (h_conv2, conv2), (h_nbrs, nbrs),
            (h_ovar, ovar), (h_oheads, oheads), (h_noise, noise),
            (h_oindex, oindex),
        ])
    ]
    for load in loads:
        load.start()

    def tell(level, to_s):
        pl.semaphore_signal(
            ready.at[level], inc=1, device_id={"space": to_s, "members": m},
            device_id_type=pl.DeviceIdType.MESH,
        )

    def tell_z(level, distance):
        tell(level, at_z(distance) * NY + y)
        tell(level, at_z(nz - distance) * NY + y)

    loads[0].wait()
    pl.semaphore_wait(gate, 4 + (NY - 1) + (nm - 1))

    fld = field_all.at[m]

    def turn(values):
        square[0:members, :] = values
        square[members : 2 * members, :] = values
        return square[...].T

    tall[8:136, :] = turn(fld[...])
    to_right = copy(tall.at[128:136], tall.at[0:8], s_halo.at[0], r_halo.at[0], right, m)
    to_left = copy(tall.at[8:16], tall.at[136:144], s_halo.at[1], r_halo.at[1], left, m)
    to_right.start()
    to_left.start()
    each(NY, lambda i: tell(0, z * NY + at_y(i)))
    tell_z(1, 1)

    def nbr_copy(i):
        return copy(nbr_all.at[m], nbr_all.at[m], s_nb.at[i], r_nb.at[i], s, at_m(i))

    def field_copy(i):
        return copy(field_all.at[m], field_all.at[m], s_fld.at[i], r_fld.at[i], s, at_m(i))

    def halo_copy(i):
        return copy(halo_all.at[m], halo_all.at[m], s_fh.at[i], r_fh.at[i], s, at_m(i))

    for load in loads[1:]:
        load.wait()
    own_row = nbrs[pl.ds(own, 1), :]
    nbr_all[m] = jnp.zeros((8, 128), I32)
    nbr_all[m, :, 0:members] = jnp.broadcast_to(own_row, (8, members))
    each(nm, lambda i: nbr_copy(i).start())

    wide = (ch, 128)
    const[0] = jnp.broadcast_to(column(gain[...], ch), wide)
    const[1] = jnp.broadcast_to(column(bias[...], ch), wide)
    const[2] = jnp.broadcast_to(column(bias1[...], ch), wide)
    const[3] = jnp.broadcast_to(column(bias2[...], ch), wide)
    read = rout[...].astype(F32).reshape(1, 3 * ch)
    const[4] = jnp.broadcast_to(column(read, ch, 2 * ch), wide)
    wcentre[0:ch, :] = conv2[1]
    wcentre[ch : ch + 16, :] = jnp.broadcast_to(read[:, 0 : 2 * ch], (16, 2 * ch)).astype(BF16)

    low = lanes((members, 128)) < half
    wide_lane = lanes((members, 128))
    low_row = lanes((1, 128)) < half
    keep_l = jnp.where(jnp.logical_and(low_row, s == 0), 0.0, 1.0)
    keep_r = jnp.where(jnp.logical_and(jnp.logical_not(low_row), s == ns - 1), 0.0, 1.0)

    def at(index):
        return pl.multiple_of(index * 128, 128)

    def lift_row(index):
        value = jnp.tanh(const[0] * fx[pl.ds(index + 5, 1), :] + const[1])
        joined[0:ch, pl.ds(at(index), 128)] = value.astype(BF16)

    def mask(top, index, keep):
        where = (slice(top, top + ch), slice(index * 128, index * 128 + 128))
        joined[where] = (joined[where].astype(F32) * keep).astype(BF16)

    def lift_inner():
        fx[8:72, :] = jnp.where(lanes((64, 128)) < half, tall[8:72, :], tall[72:136, :])

        def block(k, carry):
            for inner in range(8):
                lift_row(3 + k * 8 + inner)
            return carry

        lax.fori_loop(0, 8, block, 0)

    def lift_outer():
        near = lanes((8, 128)) < half
        fx[0:8, :] = jnp.where(near, tall[0:8, :], tall[64:72, :])
        fx[72:80, :] = jnp.where(near, tall[72:80, :], tall[136:144, :])
        for index in (0, 1, 2):
            lift_row(index)
            mask(0, index, keep_l)
        for index in (67, 68, 69):
            lift_row(index)
            mask(0, index, keep_r)

    size = STEP * 128

    def middle(block, carry=0):
        base = block * STEP
        total = dot(conv1[0], joined[0:ch, pl.ds(at(base), size)])
        total += dot(conv1[1], joined[0:ch, pl.ds(at(base + 1), size)])
        total += dot(conv1[2], joined[0:ch, pl.ds(at(base + 2), size)])
        joined[ch : 2 * ch, pl.ds(at(base + 1), size)] = silu(total + const[2][:, 0:1]).astype(BF16)
        return carry

    def last(block, carry=0):
        base = block * STEP
        centre = dot(wcentre[...], joined[:, pl.ds(at(base + 3), size)])
        total = centre[0:ch]
        total += dot(conv2[0], joined[:, pl.ds(at(base + 1), size)])
        total += dot(conv2[2], joined[:, pl.ds(at(base + 5), size)])
        third = silu(total + const[3][:, 0:1]).astype(BF16).astype(F32)
        head = centre[ch : ch + 1] + jnp.sum(third * const[4][:, 0:1], axis=0, keepdims=True)
        for inner in range(STEP):
            ht[pl.ds(base + inner, 1), :] = head[:, inner * 128 : inner * 128 + 128]
        return carry

    mids, ends = 68 // STEP, 64 // STEP

    def conv_inner():
        lax.fori_loop(1, mids - 1, middle, 0, unroll=mids - 2)
        lax.fori_loop(1, ends - 1, last, 0, unroll=ends - 2)

    def conv_outer():
        middle(0)
        middle(mids - 1)
        for index in (1, 2):
            mask(ch, index, keep_l)
        for index in (67, 68):
            mask(ch, index, keep_r)
        last(0)
        last(ends - 1)

    lift_inner()
    conv_inner()

    cell = column(oindex[...].astype(F32), slots).astype(I32)
    narrow = (slots, 3 * 64)
    of_half = jnp.bitwise_and(lanes(narrow), 63)
    cell_hot = jnp.concatenate(
        [(of_half == cell).astype(F32), (of_half + 64 == cell).astype(F32)], axis=0
    ).astype(BF16)
    pl.semaphore_wait(ready.at[1], 2)
    tell_z(2, 2)

    to_right.wait()
    to_left.wait()
    lift_outer()
    conv_outer()

    wide_obs = lanes((slots, 128))
    chosen = dot(cell_hot, jnp.concatenate(split3(ht[...]), axis=0))
    both = jnp.where(wide_obs < half, chosen[0:slots], chosen[slots : 2 * slots])
    both = both + pltpu.roll(both, half, 1)
    upper = slots // 2
    panel[y, m] = jnp.where(lanes((upper, 128)) < half, both[0:upper], both[upper:slots])

    def panel_copy(i, j):
        here = panel.at[y, m]
        return copy(here, here, s_pan.at[i, j], r_pan.at[i, j], z * NY + at_y(i), at_m(j))

    def panel_block(i):
        here = panel.at[y]
        return copy(here, here, s_pan.at[i, 0], r_pan.at[i, 0], z * NY + at_y(i), m)

    def panel_part(i, j):
        here = panel.at[y, m]
        return copy(here, here, s_pan.at[i, 0], r_pan.at[i, 0], z * NY + at_y(i), at_m(j))

    pl.semaphore_wait(ready.at[0], NY - 1)

    def all_members(i):
        def body(j, carry):
            panel_part(i, j).start()
            return carry

        lax.fori_loop(0, nm, body, 0)

    each(NY, all_members)
    each(nm, lambda j: panel_copy(0, j).start())
    variance = ovar[...]
    live = lanes((1, slots)) < h_ocount[0]
    weight = jnp.where(live, 1.0 / variance, 0.0)
    tile_t = noise[...] * column(jnp.sqrt(variance), slots) + column(oheads[...], slots)
    obs_all[y, 0, :, 0:members] = tile_t
    obs_all[y, 0, :, members : 2 * members] = tile_t
    obs_all[y, 1] = jnp.broadcast_to(column(weight, slots), (slots, 128))

    def obs_copy(i):
        return copy(obs_all.at[y], obs_all.at[y], s_ob.at[i], r_ob.at[i], z * NY + at_y(i), m)

    each(NY, lambda i: obs_copy(i).start())
    pl.semaphore_wait(ready.at[2], 2)
    tell_z(3, 4)

    each(nm, lambda j: panel_copy(0, j).wait_recv())
    each(NY, lambda i: panel_block(i).wait_recv())
    each(NY, lambda i: obs_copy(i).wait())

    depth = NY * slots
    deep = lanes((depth, 128)) < half
    packed_rows = NY * upper
    flat = [panel[:, g].reshape(packed_rows, 128) for g in range(nm)]
    swapped = [pltpu.roll(value, half, 1) for value in flat]
    front = lanes((packed_rows, 128)) < half

    def whole(first_part, second_part):
        first_part = first_part.reshape(NY, upper, 128)
        second_part = second_part.reshape(NY, upper, 128)
        return jnp.concatenate([first_part, second_part], axis=1).reshape(depth, 128)

    pairs = [
        whole(
            jnp.where(front, flat[2 * q], swapped[2 * q + 1]),
            jnp.where(front, swapped[2 * q], flat[2 * q + 1]),
        )
        for q in range(nq)
    ]
    total = pairs[0]
    for q in range(1, nq):
        total = total + pairs[q]
    centre = jnp.sum(total, axis=1, keepdims=True) / (nm * members)
    own_flat = panel[:, m].reshape(packed_rows, 128)
    own_swapped = pltpu.roll(own_flat, half, 1)
    mine = whole(
        jnp.where(front, own_flat, own_swapped), jnp.where(front, own_swapped, own_flat)
    )
    data = obs_all[:, 0].reshape(depth, 128)
    lead = obs_all[:, 1].reshape(depth, 128) * jnp.where(deep, mine - centre, data - mine)
    square[...] = lead.T
    first = pl.multiple_of(y * nz, nz)
    left_side = jnp.concatenate(
        [square[pl.ds(first, nz), :], square[pl.ds(members + first, nz), :]], axis=0
    )
    block = exact_dot(left_side, jnp.concatenate([pair - centre for pair in pairs], axis=1))
    for q in range(nq):
        tiles[:, q, :] = block[0:nz, q * 128 : q * 128 + 128]
        sides[:, q, :] = block[nz : 2 * nz, q * 128 : q * 128 + 128]

    def z_copy(i):
        return copy(tiles.at[at_z(i)], recv_z.at[i], s_z.at[i], r_z.at[i], at_z(i) * NY + y, m)

    def side_copy(i):
        return copy(sides.at[at_z(i)], recv_s.at[i], s_s.at[i], r_s.at[i], at_z(i) * NY + y, m)

    pl.semaphore_wait(ready.at[3], 2)
    each_far(lambda i: z_copy(i).start())
    each_far(lambda i: side_copy(i).start())

    own_ids = column(own_row.astype(F32), members).astype(I32)
    own_hot[...] = (lanes((members, nm * members)) == own_ids).astype(F32)
    each(nm, lambda i: nbr_copy(i).wait())
    for pair in range(nq):
        lane_ids = jnp.where(
            low_row, nbr_all[2 * pair, 0:1, :], pltpu.roll(nbr_all[2 * pair + 1], half, 1)[0:1, :]
        )
        grid = (nm * members, 128)
        onehot_col[:, pair * 128 : pair * 128 + 128] = (rows(grid) == lane_ids).astype(F32).astype(BF16)
        ids = column(lane_ids.astype(F32), 128).astype(I32)
        fold = (128, 3 * members)
        onehot_row[pair * 128 : pair * 128 + 128, :] = (
            (jnp.bitwise_and(lanes(fold), members - 1) + m * members == ids).astype(F32).astype(BF16)
        )

    each(nz, lambda i: z_copy(i).wait_recv())
    own_tile = tiles[z]
    for i in range(1, nz):
        own_tile = own_tile + recv_z[i]

    def gather_rows(buffer, sz, rz, sy, ry, meanwhile):
        def by_z(i):
            here = buffer.at[y, z]
            return copy(here, here, sz.at[i], rz.at[i], at_z(i) * NY + y, m)

        def by_y(i, row):
            here = buffer.at[y, row]
            return copy(here, here, sy.at[i], ry.at[i], z * NY + at_y(i), m)

        def block(i):
            return copy(buffer.at[y], buffer.at[y], sy.at[i], ry.at[i], z * NY + at_y(i), m)

        each_far(lambda i: by_z(i).start())
        each(NY, lambda i: by_y(i, z).start())
        result = meanwhile()

        def onward(t, carry):
            near = t // 2 + 1
            i = near + lax.rem(t, 2) * (nz - 2 * near)
            by_z(i).wait_recv()
            row = lax.rem(z + nz - i, nz)
            for k in range(1, NY):
                by_y(k, row).start()
            return carry

        lax.fori_loop(0, nz - 1, onward, 0)
        each(NY, lambda i: block(i).wait_recv())

        def sent():
            each(nz, lambda i: by_z(i).wait_send())
            each(NY, lambda i: block(i).wait_send())

        return result, sent

    def right_side():
        square[...] = jnp.zeros((128, 128), F32)
        square[0:8, :] = tall[0:8, :]
        square[8:16, :] = tall[136:144, :]
        halo_all[m] = square[...].T[0:members]
        each(nm, lambda i: field_copy(i).start())
        each(nm, lambda i: halo_copy(i).start())
        each(nz, lambda i: side_copy(i).wait_recv())
        side = sides[z]
        for i in range(1, nz):
            side = side + recv_s[i]
        value = jnp.zeros((members, 1), F32)
        for q in range(nq):
            line = jnp.broadcast_to(side[q : q + 1], (members, 128))
            value = value + jnp.sum(line * own_hot[:, q * 128 : q * 128 + 128], axis=1, keepdims=True)
        return value - jnp.mean(value, axis=0, keepdims=True)

    gram_rows[y, z] = own_tile
    rhs, gram_sent = gather_rows(gram_rows, s_gz, r_gz, s_gy, r_gy, right_side)

    parts = [split3(gram_rows[:, :, q, :].reshape(members, 128)) for q in range(nq)]
    stacked = jnp.concatenate(
        [jnp.concatenate([parts[q][k] for q in range(nq)], axis=1) for k in range(3)], axis=0
    )
    chosen = dot(stacked, onehot_col[...])
    chosen = chosen[0:members] + (chosen[members : 2 * members] + chosen[2 * members : 3 * members])
    short = members // 2
    low_short = lanes((short, 128)) < half
    for pair in range(nq):
        lump = jnp.concatenate(split3(chosen[:, pair * 128 : pair * 128 + 128]), axis=0)
        picked = dot(onehot_row[pair * 128 : pair * 128 + 128, :], lump)
        turned = pltpu.roll(picked, half, 1)
        picks[2 * pair] = jnp.where(low_short, picked[0:short], turned[short:members])
        picks[2 * pair + 1] = jnp.where(
            low_short, turned[members : members + short], picked[members + short : 2 * members]
        )

    def pick_copy(i):
        return copy(picks.at[at_m(i)], recv_m.at[i], s_a.at[i], r_a.at[i], s, at_m(i))

    each(nm, lambda i: pick_copy(i).start())
    each(nm, lambda i: pick_copy(i).wait_recv())
    packed = picks[m]
    for i in range(1, nm):
        packed = packed + recv_m[i]
    gram = jnp.concatenate([packed, pltpu.roll(packed, half, 1)], axis=0)
    gram = jnp.where(low, gram, 0.0)
    row_mean = jnp.sum(gram, axis=1, keepdims=True) / members
    col_mean = jnp.sum(gram, axis=0, keepdims=True) / members
    all_mean = jnp.sum(row_mean, axis=0, keepdims=True) / members
    gram = jnp.where(low, gram - row_mean - col_mean + all_mean, 0.0)
    gram = gram + jnp.where(wide_lane == rows((members, 128)), members - 1.0, 0.0)
    gram = jnp.where(wide_lane == members, rhs, gram)

    solved = lax.fori_loop(0, members // PIVOTS, eliminate, gram)[:, 0:1]
    coef = solved - jnp.mean(solved, axis=0, keepdims=True)
    mix = jnp.sum(own_hot[...] * coef, axis=0, keepdims=True)
    for q in range(nq):
        mix_rows[y, z, q : q + 1] = mix[:, q * 128 : q * 128 + 128]

    def arrivals():
        each(nm, lambda i: field_copy(i).wait())
        each(nm, lambda i: halo_copy(i).wait())
        each(nm, lambda j: panel_copy(0, j).wait_send())
        each(NY, lambda i: panel_block(i).wait_send())
        each(nz, lambda i: z_copy(i).wait_send())
        each(nz, lambda i: side_copy(i).wait_send())
        each(nm, lambda i: pick_copy(i).wait_send())
        gram_sent()

    _, mix_sent = gather_rows(mix_rows, s_mz, r_mz, s_my, r_my, arrivals)

    updated = fld[...]
    halos = halo_all[m]
    for q in range(nq):
        part = mix_rows[:, :, q, :].reshape(members, 128)
        updated = updated + exact_dot(part, field_all[2 * q : 2 * q + 2].reshape(128, 128))
        halos = halos + exact_dot(part, halo_all[2 * q : 2 * q + 2].reshape(128, 128))
    upd_out[...] = updated
    mix_sent()
    tall[8:136, :] = turn(updated)
    turned = turn(halos)
    tall[0:8, :] = turned[0:8, :]
    tall[136:144, :] = turned[8:16, :]
    lift_inner()
    lift_outer()
    conv_inner()
    conv_outer()
    square[0:members, :] = ht[...]
    square[members : 2 * members, :] = ht[...]
    turned = square[...].T
    head_out[...] = jnp.where(low, turned[0:members], turned[members : 2 * members])


def solution(mesh):
    ns, nm = mesh.shape["space"], mesh.shape["members"]
    nz, nq = ns // NY, nm // 2
    dma = pltpu.SemaphoreType.DMA
    vmem = pltpu.VMEM

    def on_device(
        log_field, obs_heads, obs_var, obs_noise, obs_index, obs_count, neighbours,
        lift_gain, lift_bias, conv_first, bias_first, conv_second, bias_second, readout,
    ):
        members, cells = log_field.shape
        slots = obs_var.shape[0]
        ch = lift_gain.shape[0]
        block = (members, 128)
        out = jax.ShapeDtypeStruct((members, cells), F32)
        in_vmem = pl.BlockSpec(memory_space=pltpu.VMEM)
        in_place = pl.BlockSpec(memory_space=pltpu.HBM)
        given = (
            log_field, obs_heads[None], obs_var[None], obs_noise.T, obs_index, obs_count,
            neighbours, lift_gain[None], lift_bias[None], conv_first, bias_first[None],
            conv_second, bias_second[None], readout,
        )
        scratch = [
            *[vmem(value.shape, value.dtype) for value in given[1:] if value.shape != (1,)],
            vmem((5, ch, 128), F32), vmem((ch + 16, 2 * ch), BF16), vmem((128, 128), F32),
            vmem((144, 128), F32), vmem((80, 128), F32), vmem((2 * ch, 70 * 128), BF16),
            vmem((64, 128), F32),
            vmem((nm, *block), F32), vmem((nm, *block), F32),
            vmem((nm, 8, 128), I32), vmem((nm * members, nm * members), BF16),
            vmem((nm * members, 3 * members), BF16), vmem((members, nm * members), F32),
            vmem((NY, 2, slots, 128), F32), vmem((NY, nm, slots // 2, 128), F32),
            *[vmem((nz, nq, 128), F32)] * 4,
            vmem((NY, nz, nq, 128), F32), vmem((NY, nz, nq, 128), F32),
            vmem((nm, members // 2, 128), F32), vmem((nm, members // 2, 128), F32),
            dma((len(given) - 1,)), pltpu.SemaphoreType.REGULAR((4,)), dma((2,)), dma((2,)),
            *[dma((nm,))] * 8,
            dma((NY, nm)), dma((NY, nm)),
            dma((NY,)), dma((NY,)), *[dma((nz,))] * 4,
            dma((nz,)), dma((nz,)), dma((NY,)), dma((NY,)),
            dma((nz,)), dma((nz,)), dma((NY,)), dma((NY,)),
        ]

        def body(*refs):
            kernel((ns, nm, nz), *refs)

        return pl.pallas_call(
            body,
            out_shape=(out, out),
            in_specs=[
                pl.BlockSpec(memory_space=pltpu.SMEM) if value.shape == (1,) else in_place
                for value in given
            ],
            out_specs=(in_vmem, in_vmem),
            scratch_shapes=scratch,
            name="smoother",
            compiler_params=pltpu.CompilerParams(
                collective_id=0, has_side_effects=True, vmem_limit_bytes=32 * 1024 * 1024
            ),
        )(*[
            value if value.shape == (1,) else pltpu.with_memory_space_constraint(value, pltpu.HBM)
            for value in given
        ])

    in_specs = (
        P("members", "space"), P("space"), P("space"), P("members", "space"), P("space", None),
        P("space"), P("members", None), P(), P(), P(), P(), P(), P(), P(),
    )
    out_specs = (P("members", "space"), P("members", "space"))
    return jax.shard_map(
        on_device, mesh=mesh, in_specs=in_specs, out_specs=out_specs, check_vma=False
    )
```
